256 devices in a mesh: member: 64 (over x, y, z_lo, core), lat: 4 (over z_hi).
Axes of the slice: x: 4, y: 4, z: 8 (z_hi: 4, z_lo: 2; z = z_hi * 2 + z_lo), core: 2. Of those that a mesh axis runs over, the one named last changes fastest.
Arguments:
- noisy_latents: bfloat16 [64, 64, 32, 768], P('member', 'lat'), may hold values from -6 to 6
- frames: bfloat16 [64, 64, 32, 768], P('member', 'lat'), may hold values from -6 to 6
- encoder_members: int32 [2], replicated, may hold values from 0 to 63, as said below
- window_shift: int32 [1], replicated, may hold values from 1 to 7
- encoder_in: bfloat16 [768, 768], replicated, may hold values from -0.21875 to 0.21875
- encoder_out: bfloat16 [768, 768], replicated, may hold values from -0.21875 to 0.21875
- joint_weight: bfloat16 [2304, 768], replicated, may hold values from -0.125 to 0.125
- query_weight: bfloat16 [768, 768], replicated, may hold values from -0.21875 to 0.21875
- keyvalue_weight: bfloat16 [768, 1536], replicated, may hold values from -0.21875 to 0.21875
- output_weight: bfloat16 [768, 768], replicated, may hold values from -0.21875 to 0.21875
- position_bias: float32 [12, 225], replicated, may hold values from -250 to 250
- expand_weight: bfloat16 [3072, 768], P('member'), may hold values from -0.21875 to 0.21875
- reduce_weight: bfloat16 [3072, 768], P('member'), may hold values from -0.109375 to 0.109375
Outputs:
- block_out: bfloat16 [64, 64, 32, 768], P('member', 'lat')
The draws below stay inside these ranges and needn't reach their ends.
Inputs may be any that keep to these rules, and one draw needn't show every extreme that they name: `encoder_members`: two different members, one of which is the last member, 63, in either position.
All inputs are finite; a program needn't handle non-finite values.
Results may differ from the reference program's by a relative error of at most 0.013.
Values may be sent and summed in bfloat16 or wider, within the bound.
No kernel may reach another device: no remote copies, remote signals or barrier semaphores. Data moves between devices by JAX's collectives and lax.ppermute only.
A program may use at most 128 MiB of HBM per device.

```python
import jax
import jax.numpy as jnp
import numpy as np
from jax import lax

D = 768
HD = 64
FF = 3072
WIN = 8
COLS = 32
MEMBERS = 64
NLAT = 64
H = 12


def draw_encoder_members(key, part):
    other = jax.random.randint(jax.random.fold_in(key, 11), (), 0, MEMBERS - 1).astype(jnp.int32)
    order = jax.random.randint(jax.random.fold_in(key, 12), (), 0, 2).astype(jnp.int32)
    last = jnp.array(MEMBERS - 1, jnp.int32)
    first_slot = jnp.where(order == 0, other, last)
    second_slot = jnp.where(order == 0, last, other)
    return jnp.stack([first_slot, second_slot]).astype(jnp.int32)


def draw_position_bias(key, part):
    span = 2 * WIN - 1
    base = jnp.clip(jax.random.normal(jax.random.fold_in(key, 1), (H, span * span), jnp.float32), -4.0, 4.0)
    return 0.7 * base


def block_levels(stream_key, dims, split, smallest, top_value):
    level, own = 1.0, jax.random.fold_in(stream_key, 6)
    for dim, shards_of in split:
        steps = jnp.exp(jax.random.uniform(jax.random.fold_in(own, dim), (shards_of,), jnp.float32, smallest / len(split), top_value / len(split)))
        level = level * jnp.repeat(steps, dims[dim] // shards_of).reshape([-1 if axis == dim else 1 for axis in range(len(dims))])
    return level


def centred(own_key, extent, scale, limit, pieces=(), kind=jnp.bfloat16):
    drawn = scale * jax.random.normal(own_key, extent, jnp.float32)
    if pieces:
        drawn = drawn * block_levels(own_key, extent, pieces, -0.22, 0.18)
    return jnp.clip(drawn, -limit, limit).astype(kind)


def setup_inputs(seed: int = 0) -> dict:
    streams_of = jax.random.split(jax.random.key(seed), 14)
    return {
        "noisy_latents": centred(streams_of[0], (MEMBERS, NLAT, COLS, D), 1.0, 6.0, ((0, 64), (1, 4))),
        "frames": centred(streams_of[1], (MEMBERS, NLAT, COLS, D), 1.0, 6.0, ((0, 64), (1, 4))),
        "encoder_members": draw_encoder_members(jax.random.fold_in(streams_of[13], 71), 0),
        "window_shift": jax.random.randint(streams_of[3], (1,), 1, WIN).astype(jnp.int32),
        "encoder_in": centred(streams_of[4], (D, D), D ** -0.5, 0.21875),
        "encoder_out": centred(streams_of[5], (D, D), D ** -0.5, 0.21875),
        "joint_weight": centred(streams_of[6], (3 * D, D), (3 * D) ** -0.5, 0.125),
        "query_weight": centred(streams_of[7], (D, D), D ** -0.5, 0.21875),
        "keyvalue_weight": centred(streams_of[8], (D, 2 * D), D ** -0.5, 0.21875),
        "output_weight": centred(streams_of[9], (D, D), D ** -0.5, 0.21875),
        "position_bias": draw_position_bias(jax.random.fold_in(streams_of[13], 71), 0),
        "expand_weight": centred(streams_of[11], (FF, D), D ** -0.5, 0.21875, ((0, 64),)),
        "reduce_weight": centred(streams_of[12], (FF, D), FF ** -0.5, 0.109375, ((0, 64),)),
    }


epsilon = 1e-06

def offset_table(win):
    position = np.arange(win * win)
    row_pos = position // win
    col_pos = position % win
    row_diff = row_pos[None, :] - row_pos[:, None] + win - 1
    col_diff = col_pos[None, :] - col_pos[:, None] + win - 1
    return (row_diff * (2 * win - 1) + col_diff).astype(np.int32)

def rms_norm(values):
    scale = lax.rsqrt(lax.optimization_barrier(jnp.mean(values * values, axis=-1, keepdims=True)) + epsilon)
    return (values * scale).astype(jnp.bfloat16)

def encode(frame, encoder_in, encoder_out):
    hidden = jax.nn.gelu(jnp.dot(frame, encoder_in, preferred_element_type=jnp.float32)).astype(jnp.bfloat16)
    return jnp.dot(hidden, encoder_out, preferred_element_type=jnp.float32).astype(jnp.bfloat16)

def window_attention(query, key_rows, value_rows, valid, position_bias, shift):
    nrows, ncols, width = query.shape
    heads = width // HD
    row_groups, col_groups = (nrows // WIN, ncols // WIN)

    def arrange(block):
        block = jnp.roll(block, shift, axis=1)
        block = block.reshape(row_groups, WIN, col_groups, WIN, heads, HD)
        return block.transpose(0, 2, 4, 1, 3, 5).reshape(row_groups * col_groups, heads, WIN * WIN, HD)
    query_win = arrange(query).astype(jnp.float32)
    key_win = arrange(key_rows).astype(jnp.float32)
    value_win = arrange(value_rows).astype(jnp.float32)
    keep = jnp.broadcast_to(valid.reshape(row_groups, 1, WIN, 1), (row_groups, col_groups, WIN, WIN))
    keep = keep.reshape(row_groups * col_groups, 1, 1, WIN * WIN)
    bias = position_bias[:, offset_table(WIN)]
    scores = jnp.einsum('whqd,whkd->whqk', query_win, key_win) * HD ** (-0.5) + bias[None]
    scores = jnp.where(keep, scores, -1e+30)
    highest = lax.optimization_barrier(jnp.max(scores, axis=-1, keepdims=True))
    weights = jnp.exp(scores - highest)
    probs = (weights / lax.optimization_barrier(jnp.sum(weights, axis=-1, keepdims=True))).astype(jnp.bfloat16)
    mixed = jnp.einsum('whqk,whkd->whqd', probs.astype(jnp.float32), value_win).astype(jnp.bfloat16)
    mixed = mixed.reshape(row_groups, col_groups, heads, WIN, WIN, HD).transpose(0, 3, 1, 4, 2, 5)
    return jnp.roll(mixed.reshape(nrows, ncols, width), -shift, axis=1)

def reference(noisy_latents, frames, encoder_members, window_shift, encoder_in, encoder_out, joint_weight, query_weight, keyvalue_weight, output_weight, position_bias, expand_weight, reduce_weight):
    shift = window_shift[0]
    width = noisy_latents.shape[-1]
    margin = WIN // 2
    first = encode(frames[encoder_members[0]], encoder_in, encoder_out)
    second = encode(frames[encoder_members[1]], encoder_in, encoder_out)
    cond_term = jnp.dot(first, joint_weight[width:2 * width], preferred_element_type=jnp.float32)
    cond_term = cond_term + jnp.dot(second, joint_weight[2 * width:], preferred_element_type=jnp.float32)
    valid = jnp.concatenate([jnp.zeros((margin,), bool), jnp.ones((NLAT,), bool), jnp.zeros((margin,), bool)])

    def one_member(noisy_member):
        stream = (jnp.dot(noisy_member, joint_weight[:width], preferred_element_type=jnp.float32) + cond_term).astype(jnp.bfloat16)
        normed = rms_norm(stream.astype(jnp.float32))
        query = jnp.dot(normed, query_weight, preferred_element_type=jnp.float32).astype(jnp.bfloat16)
        keyvalue = jnp.dot(normed, keyvalue_weight, preferred_element_type=jnp.float32).astype(jnp.bfloat16)
        padding = ((margin, margin), (0, 0), (0, 0))
        query_pad = jnp.pad(query, padding)
        keyvalue_pad = jnp.pad(keyvalue, padding)
        mixed = window_attention(query_pad, keyvalue_pad[..., :width], keyvalue_pad[..., width:], valid, position_bias, shift)[margin:margin + NLAT]
        attended = (stream.astype(jnp.float32) + jnp.dot(mixed, output_weight, preferred_element_type=jnp.float32)).astype(jnp.bfloat16)
        second_normed = rms_norm(attended.astype(jnp.float32))
        hidden = jax.nn.gelu(jnp.dot(second_normed, expand_weight.T, preferred_element_type=jnp.float32)).astype(jnp.bfloat16)
        update = jnp.dot(hidden, reduce_weight, preferred_element_type=jnp.float32)
        return (attended.astype(jnp.float32) + update).astype(jnp.bfloat16)
    return lax.map(one_member, noisy_latents)
```

```python
import jax
import jax.numpy as jnp
import numpy as np
from jax import lax
from jax.experimental import pallas as pl
from jax.experimental.pallas import tpu as pltpu
from jax.sharding import Mesh
from jax.sharding import PartitionSpec as P

HD = 64
WIN = 8
D = 768
H = 12
FF = 3072
ROWS = 16
COLS = 32
GROUPS = 3
MEMBER = ("mx", "my", "mz", "core")
PLANE = ("mx", "my")
EPS = 1e-06
F32 = jnp.float32
BF16 = jnp.bfloat16


def dot(a, b):
    return jnp.dot(a, b, preferred_element_type=F32)


def dot_nt(a, b):
    return lax.dot_general(a, b, (((1,), (1,)), ((), ())), preferred_element_type=F32)


def dot_tn(a, b):
    return lax.dot_general(a, b, (((0,), (0,)), ((), ())), preferred_element_type=F32)


def normalised(x):
    scale = lax.rsqrt(jnp.mean(x * x, axis=-1, keepdims=True) + EPS)
    return (x * scale).astype(BF16)


def one_hot(wanted, width):
    lanes = lax.broadcasted_iota(jnp.int32, (wanted.shape[0], width), 1)
    return jnp.where(lanes == wanted, 1.0, 0.0).astype(BF16)


def row_ids(count):
    return lax.broadcasted_iota(jnp.int32, (count, 1), 0)


def window_place(count, shift):
    t = row_ids(count)
    row = (t // WIN) % WIN
    col = ((t // (WIN * WIN)) * WIN + t % WIN - shift + COLS) % COLS
    return row, col


def encode_kernel(scal, frame_hbm, in_hbm, out_hbm, joint_hbm, keep_ref, send_ref, frame, w_in, w_out, w_slot, sems):
    copies = [
        pltpu.make_async_copy(frame_hbm, frame, sems.at[0]),
        pltpu.make_async_copy(in_hbm, w_in, sems.at[1]),
        pltpu.make_async_copy(out_hbm, w_out, sems.at[2]),
        pltpu.make_async_copy(joint_hbm.at[pl.ds(pl.multiple_of(scal[1] * D, D), D), :], w_slot, sems.at[3]),
    ]
    for c in copies:
        c.start()
    tokens = ROWS * COLS
    t = row_ids(tokens)
    half = tokens // 2
    core = jnp.where(t < half, scal[2], 1 - scal[2])
    col = core * (COLS // 2) + (t % half) // ROWS
    order = one_hot((t % ROWS) * COLS + col, tokens)
    copies[0].wait()
    ordered = dot(order, frame[...]).astype(BF16)
    copies[1].wait()
    hidden = jax.nn.gelu(dot(ordered, w_in[...])).astype(BF16)
    copies[2].wait()
    condition = dot(hidden, w_out[...]).astype(BF16)
    copies[3].wait()
    term = dot(condition, w_slot[...])
    term = jnp.where(scal[0] > 0, term, 0.0).astype(BF16)
    keep_ref[...] = term[:half]
    send_ref[...] = term[half:]


def encode(scal, frame, w_in, w_out, joint):
    tokens = ROWS * COLS
    any_spec = pl.BlockSpec(memory_space=pl.ANY)
    out = jax.ShapeDtypeStruct((tokens // 2, D), BF16)
    return pl.pallas_call(
        encode_kernel,
        name="encode",
        in_specs=[pl.BlockSpec(memory_space=pltpu.SMEM)] + [any_spec] * 4,
        out_shape=(out, out),
        scratch_shapes=[
            pltpu.VMEM((tokens, D), BF16),
            pltpu.VMEM((D, D), BF16),
            pltpu.VMEM((D, D), BF16),
            pltpu.VMEM((D, D), BF16),
            pltpu.SemaphoreType.DMA((4,)),
        ],
        compiler_params=pltpu.CompilerParams(vmem_limit_bytes=32 << 20),
        cost_estimate=pl.CostEstimate(flops=2 * tokens * D * (3 * D + tokens), bytes_accessed=6_000_000, transcendentals=tokens * D),
    )(scal, frame, w_in, w_out, joint)


def noisy_kernel(scal, up_ref, own_ref, down_ref, w_ref, out_ref):
    row, col = window_place(256, scal[0])
    order = one_hot(row * COLS + col, 256)
    tokens = jnp.concatenate([up_ref[...], own_ref[...], down_ref[...]], axis=0)
    for g in range(GROUPS):
        placed = dot(order, tokens[g * 256 : (g + 1) * 256]).astype(BF16)
        out_ref[g] = dot(placed, w_ref[...])


def noisy_share(scal, up, own, down, joint):
    vmem = pl.BlockSpec(memory_space=pltpu.VMEM)
    return pl.pallas_call(
        noisy_kernel,
        name="noisy_share",
        grid=(1,),
        in_specs=[
            pl.BlockSpec(memory_space=pltpu.SMEM),
            vmem,
            vmem,
            vmem,
            pl.BlockSpec((D, D), lambda i: (0, 0)),
        ],
        out_specs=vmem,
        out_shape=jax.ShapeDtypeStruct((GROUPS, 256, D), F32),
        compiler_params=pltpu.CompilerParams(vmem_limit_bytes=32 << 20),
        cost_estimate=pl.CostEstimate(flops=2 * 768 * D * (D + 256), bytes_accessed=5_000_000, transcendentals=0),
    )(scal, up, own, down, joint)


def attend_kernel(scal, noisy_ref, mine_ref, other_ref, strip_ref, wq_ref, wkv_ref, wo_ref, out_ref, bias_ref, qkv_ref, mixed_ref):
    shift = scal[0]
    core = scal[1]
    band = scal[2]
    last = scal[3]
    for h in range(H):
        for r in range(WIN):
            at = WIN * (WIN - 1 - r)
            bias_ref[h // 2, WIN * r : WIN * (r + 1), (h % 2) * HD : (h % 2 + 1) * HD] = strip_ref[h, :, at : at + HD]
    row, col = window_place(256, shift)
    half = COLS // 2
    place = (col % half) * WIN + row
    from_mine = one_hot(jnp.where(col // half == core, place, -1), 128)
    from_other = one_hot(jnp.where(col // half == core, -1, place), 128)
    low = lax.broadcasted_iota(jnp.int32, (64, 128), 1) < HD
    key_row = lax.broadcasted_iota(jnp.int32, (64, 128), 0)
    done = 0
    for g in range(GROUPS):
        mine = mine_ref[:, g * WIN : (g + 1) * WIN, :].astype(F32).reshape(128, D).astype(BF16)
        other = other_ref[:, g * WIN : (g + 1) * WIN, :].astype(F32).reshape(128, D).astype(BF16)
        stream = (noisy_ref[g] + (dot(from_mine, mine) + dot(from_other, other))).astype(BF16)
        normed = normalised(stream.astype(F32))
        qkv_ref[:, :D] = dot(normed, wq_ref[...]).astype(BF16)
        qkv_ref[:, D:] = dot(normed, wkv_ref[...]).astype(BF16)
        for w in range(4):
            rows = slice(w * 64, (w + 1) * 64)
            for p in range(H // 2):
                q = qkv_ref[rows, p * 128 : (p + 1) * 128]
                k = qkv_ref[rows, D + p * 128 : D + (p + 1) * 128]
                v = qkv_ref[rows, 2 * D + p * 128 : 2 * D + (p + 1) * 128]
                zero = jnp.zeros_like(q)
                both = jnp.concatenate([jnp.where(low, q, zero), jnp.where(low, zero, q)], axis=0)
                scores = dot_nt(k, both) * HD ** (-0.5) + bias_ref[p]
                if g == 0:
                    scores = jnp.where(jnp.logical_and(band == 0, key_row < 32), -1e30, scores)
                if g == GROUPS - 1:
                    scores = jnp.where(jnp.logical_and(band == last, key_row >= 32), -1e30, scores)
                weights = jnp.exp(scores - jnp.max(scores, axis=0, keepdims=True))
                probs = (weights * (1.0 / jnp.sum(weights, axis=0, keepdims=True))).astype(BF16)
                got = dot_tn(probs, v)
                mixed_ref[rows, p * 128 : (p + 1) * 128] = jnp.where(low, got[:64], got[64:]).astype(BF16)
        count, first = ((128, 4), (256, 0), (128, 0))[g]
        t = row_ids(count)
        moved = (t % COLS + shift) % COLS
        back = one_hot((moved // WIN) * 64 + (t // COLS + first) * WIN + moved % WIN, 256)
        mixed = dot(back, mixed_ref[...]).astype(BF16)
        out_ref[done : done + count, :] = (dot(back, stream) + dot(mixed, wo_ref[...])).astype(BF16)
        done += count


def attend(scal, noisy, mine, other, strip, wq, wkv, wo):
    vmem = pl.BlockSpec(memory_space=pltpu.VMEM)
    return pl.pallas_call(
        attend_kernel,
        name="attend",
        in_specs=[pl.BlockSpec(memory_space=pltpu.SMEM)] + [vmem] * 7,
        out_specs=vmem,
        out_shape=jax.ShapeDtypeStruct((ROWS * COLS, D), BF16),
        scratch_shapes=[
            pltpu.VMEM((H // 2, 64, 128), F32),
            pltpu.VMEM((256, 3 * D), BF16),
            pltpu.VMEM((256, D), BF16),
        ],
        compiler_params=pltpu.CompilerParams(vmem_limit_bytes=40 << 20),
        cost_estimate=pl.CostEstimate(flops=2 * 768 * D * 5 * D, bytes_accessed=10_000_000, transcendentals=768 * 64 * 12),
    )(scal, noisy, mine, other, strip, wq, wkv, wo)


def forward_kernel(count, att_ref, *refs):
    pieces = refs[:count]
    out_ref = refs[count]
    weights, total, sems = refs[count + 1 :]
    size = FF // count
    copies = [pltpu.make_async_copy(pieces[i], weights.at[pl.ds(i * size, size), :], sems.at[i]) for i in range(count)]
    for c in copies:
        c.start()
    x = att_ref[...].astype(F32)
    second = normalised(x)
    total[...] = x
    chunk = 768
    per = chunk // size
    for j in range(FF // chunk):
        for c in copies[j * per : (j + 1) * per]:
            c.wait()
        rows = slice(j * chunk, (j + 1) * chunk)
        hidden = jax.nn.gelu(dot_nt(second, weights[rows, :D])).astype(BF16)
        total[...] += dot(hidden, weights[rows, D:])
    out_ref[...] = total[...].astype(BF16)


def feed_forward(att, pieces):
    tokens = ROWS * COLS
    count = len(pieces)
    vmem = pl.BlockSpec(memory_space=pltpu.VMEM)
    return pl.pallas_call(
        lambda *refs: forward_kernel(count, *refs),
        name="feed_forward",
        in_specs=[vmem] + [pl.BlockSpec(memory_space=pl.ANY)] * count,
        out_specs=vmem,
        out_shape=jax.ShapeDtypeStruct((tokens, D), BF16),
        scratch_shapes=[
            pltpu.VMEM((FF, 2 * D), BF16),
            pltpu.VMEM((tokens, D), F32),
            pltpu.SemaphoreType.DMA((count,)),
        ],
        compiler_params=pltpu.CompilerParams(vmem_limit_bytes=40 << 20),
        cost_estimate=pl.CostEstimate(flops=4 * tokens * D * FF, bytes_accessed=12_000_000, transcendentals=tokens * FF),
    )(att, *pieces)


def swap(x, axis):
    return lax.ppermute(x, axis, [(0, 1), (1, 0)])


HALVES = {"a": [(0, 1), (1, 0), (2, 3), (3, 2)], "b": [(1, 2), (2, 1), (3, 0), (0, 3)]}
STEPS = (("mx", "a"), ("my", "a"), ("mx", "b"), ("my", "b"))


def gathered_weights(expand, reduce):
    own = jnp.concatenate([expand, reduce], axis=1)
    across = swap(own, "mz")
    n = own.shape[0] // 2
    held = [own[:n], own[n:], across[:n], across[n:]]
    pieces = []
    for step in range(4):
        got = []
        for k in range(4):
            axis, kind = STEPS[(k + step) % 4]
            got.append(lax.ppermute(held[k], axis, HALVES[kind]))
        if step < 3:
            held = [jnp.concatenate([a, b], axis=0) for a, b in zip(held, got)]
        else:
            pieces = held + got
    return pieces + [swap(p, "core") for p in pieces]


def strip_choice():
    lane = lax.optimization_barrier(jnp.arange(WIN * 15 * WIN))
    key_col = lane // (15 * WIN)
    block = lane // WIN % 15
    wanted = (14 - block) * 15 + key_col - lane % WIN + 7
    return jnp.where(jnp.arange(225)[:, None] == wanted[None, :], 1.0, 0.0).astype(F32)


def per_device(
    noisy_latents,
    frames,
    encoder_members,
    window_shift,
    encoder_in,
    encoder_out,
    joint_weight,
    query_weight,
    keyvalue_weight,
    output_weight,
    position_bias,
    expand_weight,
    reduce_weight,
):
    tokens = ROWS * COLS
    margin = WIN // 2
    bands = lax.axis_size("lat")
    member = lax.axis_index(MEMBER)
    core = lax.axis_index("core")
    is_second = member == encoder_members[1]
    is_source = jnp.logical_or(member == encoder_members[0], is_second)
    shift = window_shift[0]
    noisy = noisy_latents.reshape(tokens, D)
    down_pairs = [(i, i + 1) for i in range(bands - 1)]
    up_pairs = [(i + 1, i) for i in range(bands - 1)]
    edge = margin * COLS

    enc_scal = jnp.stack([is_source.astype(jnp.int32), 1 + is_second.astype(jnp.int32), core])
    keep, send = encode(enc_scal, frames.reshape(tokens, D), encoder_in, encoder_out, joint_weight)

    noisy_up = lax.ppermute(noisy[tokens - edge :], "lat", down_pairs)
    noisy_down = lax.ppermute(noisy[:edge], "lat", up_pairs)
    pieces = gathered_weights(expand_weight, reduce_weight)

    mine = (keep + swap(send, "core")).reshape(COLS // 2, ROWS, D)
    spread = lax.all_to_all(mine, PLANE, 0, 0, tiled=True)
    part = jnp.sum(spread.astype(F32), axis=0).astype(BF16)
    above = lax.ppermute(part[ROWS - margin :], "lat", down_pairs)
    below = lax.ppermute(part[:margin], "lat", up_pairs)
    part = jnp.concatenate([above, part, below], axis=0)
    part = part + swap(part, "mz")
    mine = lax.all_to_all(jnp.broadcast_to(part[None], (COLS // 2, *part.shape)), PLANE, 0, 0, tiled=True)
    other = swap(mine, "core")

    noisy_wide = noisy_share(jnp.stack([shift, shift]), noisy_up, noisy, noisy_down, joint_weight)
    strip = jnp.dot(position_bias, strip_choice(), precision=lax.Precision.HIGHEST, preferred_element_type=F32)
    strip = strip.reshape(H, WIN, 15 * WIN)
    att_scal = jnp.stack([shift, core, lax.axis_index("lat"), jnp.int32(bands - 1)])
    attended = attend(att_scal, noisy_wide, mine, other, strip, query_weight, keyvalue_weight, output_weight)
    return feed_forward(attended, pieces).reshape(noisy_latents.shape)


def solution(mesh):
    finer = Mesh(mesh.devices.reshape(4, 4, 2, 2, mesh.shape["lat"]), (*MEMBER, "lat"))
    placed = (
        P(MEMBER, "lat", None, None),
        P(MEMBER, "lat", None, None),
        *([P()] * 9),
        P(MEMBER, None),
        P(MEMBER, None),
    )
    return jax.shard_map(
        per_device,
        mesh=finer,
        in_specs=placed,
        out_specs=P(MEMBER, "lat", None, None),
        check_vma=False,
    )
```

```python
import jax
import jax.numpy as jnp
from jax import lax
from jax.experimental import pallas as pl
from jax.experimental.pallas import tpu as pltpu
from jax.sharding import Mesh
from jax.sharding import PartitionSpec as P

HD = 64
WIN = 8
D = 768
H = 12
FF = 3072
ROWS = 16
COLS = 32
GROUPS = 3
MEMBER = ("mx", "my", "mz", "core")
PLANE = ("mx", "my")
EPS = 1e-06
F32 = jnp.float32
BF16 = jnp.bfloat16
GRANT = 64_000_000


def dot(a, b):
    return jnp.dot(a, b, preferred_element_type=F32)


def dot_nt(a, b):
    return lax.dot_general(a, b, (((1,), (1,)), ((), ())), preferred_element_type=F32)


def dot_tn(a, b):
    return lax.dot_general(a, b, (((0,), (0,)), ((), ())), preferred_element_type=F32)


def normalised(x):
    scale = lax.rsqrt(jnp.mean(x * x, axis=-1, keepdims=True) + EPS)
    return (x * scale).astype(BF16)


def one_hot(wanted, width):
    lanes = lax.broadcasted_iota(jnp.int32, (wanted.shape[0], width), 1)
    return jnp.where(lanes == wanted, 1.0, 0.0).astype(BF16)


def row_ids(count):
    return lax.broadcasted_iota(jnp.int32, (count, 1), 0)


def window_place(count, shift):
    t = row_ids(count)
    row = (t // WIN) % WIN
    col = ((t // (WIN * WIN)) * WIN + t % WIN - shift + COLS) % COLS
    return row, col


def encode_kernel(scal, frame_hbm, in_hbm, out_hbm, joint_hbm, keep_ref, send_ref, frame, w_in, w_out, w_slot, sems):
    copies = [
        pltpu.make_async_copy(frame_hbm, frame, sems.at[0]),
        pltpu.make_async_copy(in_hbm, w_in, sems.at[1]),
        pltpu.make_async_copy(out_hbm, w_out, sems.at[2]),
        pltpu.make_async_copy(joint_hbm.at[pl.ds(pl.multiple_of(scal[1] * D, D), D), :], w_slot, sems.at[3]),
    ]
    for c in copies:
        c.start()
    tokens = ROWS * COLS
    t = row_ids(tokens)
    half = tokens // 2
    core = jnp.where(t < half, scal[2], 1 - scal[2])
    col = core * (COLS // 2) + (t % half) // ROWS
    order = one_hot((t % ROWS) * COLS + col, tokens)
    copies[0].wait()
    ordered = dot(order, frame[...]).astype(BF16)
    copies[1].wait()
    hidden = jax.nn.gelu(dot(ordered, w_in[...])).astype(BF16)
    copies[2].wait()
    condition = dot(hidden, w_out[...]).astype(BF16)
    copies[3].wait()
    term = dot(condition, w_slot[...])
    term = jnp.where(scal[0] > 0, term, 0.0).astype(BF16)
    keep_ref[...] = term[:half]
    send_ref[...] = term[half:]


def encode(scal, frame, w_in, w_out, joint):
    tokens = ROWS * COLS
    any_spec = pl.BlockSpec(memory_space=pl.ANY)
    out = jax.ShapeDtypeStruct((tokens // 2, D), BF16)
    return pl.pallas_call(
        encode_kernel,
        name="encode",
        in_specs=[pl.BlockSpec(memory_space=pltpu.SMEM)] + [any_spec] * 4,
        out_shape=(out, out),
        scratch_shapes=[
            pltpu.VMEM((tokens, D), BF16),
            pltpu.VMEM((D, D), BF16),
            pltpu.VMEM((D, D), BF16),
            pltpu.VMEM((D, D), BF16),
            pltpu.SemaphoreType.DMA((4,)),
        ],
        compiler_params=pltpu.CompilerParams(vmem_limit_bytes=GRANT),
        cost_estimate=pl.CostEstimate(flops=2 * tokens * D * (3 * D + tokens), bytes_accessed=6_000_000, transcendentals=tokens * D),
    )(scal, frame, w_in, w_out, joint)


def noisy_kernel(scal, up_hbm, own_hbm, down_hbm, joint_hbm, out_ref, tokens, weight, sems):
    edge = up_hbm.shape[0]
    own = own_hbm.shape[0]
    copies = [
        pltpu.make_async_copy(joint_hbm.at[pl.ds(0, D), :], weight, sems.at[0]),
        pltpu.make_async_copy(up_hbm, tokens.at[pl.ds(0, edge), :], sems.at[1]),
        pltpu.make_async_copy(own_hbm, tokens.at[pl.ds(edge, own), :], sems.at[2]),
        pltpu.make_async_copy(down_hbm, tokens.at[pl.ds(edge + own, edge), :], sems.at[3]),
    ]
    for c in copies:
        c.start()
    row, col = window_place(256, scal[0])
    order = one_hot(row * COLS + col, 256)
    for c in copies:
        c.wait()
    for g in range(GROUPS):
        placed = dot(order, tokens[g * 256 : (g + 1) * 256, :]).astype(BF16)
        out_ref[g] = dot(placed, weight[...])


def noisy_share(scal, up, own, down, joint):
    any_spec = pl.BlockSpec(memory_space=pl.ANY)
    return pl.pallas_call(
        noisy_kernel,
        name="noisy_share",
        in_specs=[pl.BlockSpec(memory_space=pltpu.SMEM)] + [any_spec] * 4,
        out_specs=pl.BlockSpec(memory_space=pltpu.VMEM),
        out_shape=jax.ShapeDtypeStruct((GROUPS, 256, D), F32),
        scratch_shapes=[
            pltpu.VMEM((768, D), BF16),
            pltpu.VMEM((D, D), BF16),
            pltpu.SemaphoreType.DMA((4,)),
        ],
        compiler_params=pltpu.CompilerParams(vmem_limit_bytes=GRANT),
        cost_estimate=pl.CostEstimate(flops=2 * 768 * D * (D + 256), bytes_accessed=5_000_000, transcendentals=0),
    )(scal, up, own, down, joint)


def attend_kernel(scal, noisy_hbm, mine_hbm, other_hbm, strip_hbm, wq_hbm, wkv_hbm, wo_hbm, out_ref, bias_ref, stream_ref, normed_ref, qkv_ref, mixed_ref, wqkv, wo, noisy_ref, mine_ref, other_ref, strip_ref, sems):
    copies = [
        pltpu.make_async_copy(wq_hbm, wqkv.at[:, :D], sems.at[0]),
        pltpu.make_async_copy(wkv_hbm, wqkv.at[:, D:], sems.at[1]),
        pltpu.make_async_copy(wo_hbm, wo, sems.at[2]),
    ]
    early = [
        pltpu.make_async_copy(strip_hbm, strip_ref, sems.at[3]),
        pltpu.make_async_copy(mine_hbm, mine_ref, sems.at[4]),
        pltpu.make_async_copy(other_hbm, other_ref, sems.at[5]),
        pltpu.make_async_copy(noisy_hbm, noisy_ref, sems.at[6]),
    ]
    for c in early + copies:
        c.start()
    early[0].wait()
    shift = scal[0]
    core = scal[1]
    band = scal[2]
    last = scal[3]
    pairs = H // 2
    for h in range(H):
        for r in range(WIN):
            at = WIN * (WIN - 1 - r)
            bias_ref[h // 2, WIN * r : WIN * (r + 1), (h % 2) * HD : (h % 2 + 1) * HD] = strip_ref[h, :, at : at + HD]
    row, col = window_place(256, shift)
    half = COLS // 2
    place = (col % half) * WIN + row
    from_mine = one_hot(jnp.where(col // half == core, place, -1), 128)
    from_other = one_hot(jnp.where(col // half == core, -1, place), 128)
    for c in early[1:]:
        c.wait()
    for g in range(GROUPS):
        mine = mine_ref[:, g * WIN : (g + 1) * WIN, :].astype(F32).reshape(128, D).astype(BF16)
        other = other_ref[:, g * WIN : (g + 1) * WIN, :].astype(F32).reshape(128, D).astype(BF16)
        stream = (noisy_ref[g] + (dot(from_mine, mine) + dot(from_other, other))).astype(BF16)
        stream_ref[g * 256 : (g + 1) * 256, :] = stream
        normed_ref[g * 256 : (g + 1) * 256, :] = normalised(stream.astype(F32))
    copies[0].wait()
    copies[1].wait()
    for n in range(3):
        cols = slice(n * D, (n + 1) * D)
        qkv_ref[:, cols] = dot(normed_ref[...], wqkv[:, cols]).astype(BF16)
    low = lax.broadcasted_iota(jnp.int32, (64, 128), 1) < HD
    key_row = lax.broadcasted_iota(jnp.int32, (64, 128), 0)

    def window(w, carry):
        rows = pl.ds(pl.multiple_of(w * 64, 64), 64)
        hide_top = jnp.logical_and(w < 4, band == 0)
        hide_end = jnp.logical_and(w >= 8, band == last)
        first = jnp.where(hide_top, 32, 0)
        end = jnp.where(hide_end, 32, 64)
        seen = jnp.logical_and(key_row >= first, key_row < end)
        scores = []
        for p in range(pairs):
            q = qkv_ref[rows, p * 128 : (p + 1) * 128]
            k = qkv_ref[rows, D + p * 128 : D + (p + 1) * 128]
            zero = jnp.zeros_like(q)
            both = jnp.concatenate([jnp.where(low, q, zero), jnp.where(low, zero, q)], axis=0)
            scores.append(dot_nt(k, both))
        scores = [jnp.where(seen, s * HD ** (-0.5) + bias_ref[p], -1e30) for p, s in enumerate(scores)]
        tops = [jnp.max(s, axis=0, keepdims=True) for s in scores]
        weights = [jnp.exp(s - m) for s, m in zip(scores, tops)]
        sums = [1.0 / jnp.sum(e, axis=0, keepdims=True) for e in weights]
        probs = [(e * i).astype(BF16) for e, i in zip(weights, sums)]
        got = [dot_tn(probs[p], qkv_ref[rows, 2 * D + p * 128 : 2 * D + (p + 1) * 128]) for p in range(pairs)]
        for p in range(pairs):
            mixed_ref[rows, p * 128 : (p + 1) * 128] = jnp.where(low, got[p][:64], got[p][64:]).astype(BF16)
        return carry

    lax.fori_loop(0, 4 * GROUPS, window, 0, unroll=2)
    t = row_ids(128)
    moved = (t % COLS + shift) % COLS
    base = (moved // WIN) * 64 + (t // COLS) * WIN + moved % WIN
    for b in range(4):
        g, first = divmod(4 * b + 4, WIN)
        back = one_hot(base + first * WIN, 256)
        mixed = dot(back, mixed_ref[g * 256 : (g + 1) * 256, :]).astype(BF16)
        normed_ref[b * 128 : (b + 1) * 128, :] = mixed
        qkv_ref[b * 128 : (b + 1) * 128, :D] = dot(back, stream_ref[g * 256 : (g + 1) * 256, :]).astype(BF16)
    copies[2].wait()
    tokens = ROWS * COLS
    out_ref[...] = (qkv_ref[:tokens, :D].astype(F32) + dot(normed_ref[:tokens, :], wo[...])).astype(BF16)


def attend(scal, noisy, mine, other, strip, wq, wkv, wo):
    vmem = pl.BlockSpec(memory_space=pltpu.VMEM)
    any_spec = pl.BlockSpec(memory_space=pl.ANY)
    return pl.pallas_call(
        attend_kernel,
        name="attend",
        in_specs=[pl.BlockSpec(memory_space=pltpu.SMEM)] + [any_spec] * 7,
        out_specs=vmem,
        out_shape=jax.ShapeDtypeStruct((ROWS * COLS, D), BF16),
        scratch_shapes=[
            pltpu.VMEM((H // 2, 64, 128), F32),
            pltpu.VMEM((768, D), BF16),
            pltpu.VMEM((768, D), BF16),
            pltpu.VMEM((768, 3 * D), BF16),
            pltpu.VMEM((768, D), BF16),
            pltpu.VMEM((D, 3 * D), BF16),
            pltpu.VMEM((D, D), BF16),
            pltpu.VMEM(noisy.shape, F32),
            pltpu.VMEM(mine.shape, BF16),
            pltpu.VMEM(other.shape, BF16),
            pltpu.VMEM(strip.shape, F32),
            pltpu.SemaphoreType.DMA((7,)),
        ],
        compiler_params=pltpu.CompilerParams(vmem_limit_bytes=GRANT),
        cost_estimate=pl.CostEstimate(flops=2 * 768 * D * 5 * D, bytes_accessed=10_000_000, transcendentals=768 * 64 * 12),
    )(scal, noisy, mine, other, strip, wq, wkv, wo)


def forward_kernel(keep, att_hbm, *refs):
    ups = refs[0:5]
    downs = refs[5:10]
    out_ref, up, down, total, att_ref, sems = refs[10:]
    taken = pltpu.make_async_copy(att_hbm, att_ref, sems.at[40])
    taken.start()
    unit = 96
    copies = []
    for i in range(4):
        for j in range(4):
            slot = 4 * i + j
            pair = []
            for side, (pieces, held, far, at) in enumerate(((ups, up, i, j), (downs, down, j, i))):
                sem = sems.at[2 * slot + side]
                if far < 3:
                    pair.append(pltpu.make_async_copy(pieces[far].at[at], held.at[pl.ds(slot * unit, unit), :], sem))
                else:
                    h = unit // 2
                    pair.append(pltpu.make_async_copy(pieces[3].at[at], held.at[pl.ds(slot * unit, h), :], sem))
                    pair.append(pltpu.make_async_copy(pieces[4].at[at], held.at[pl.ds(slot * unit + h, h), :], sems.at[32 + 2 * (j if side == 0 else i) + side]))
            for c in pair:
                c.start()
            copies.append(pair)
    taken.wait()
    x = att_ref[...].astype(F32)
    second = normalised(x)
    for n in range(2):
        for pair in copies[8 * n : 8 * n + 8]:
            for c in pair:
                c.wait()
        rows = slice(n * 768, (n + 1) * 768)
        hidden = jax.nn.gelu(dot_nt(second, up[rows, :])).astype(BF16)
        part = dot(hidden, down[rows, :])
        if n == 0:
            total[...] = x + part if keep else part
        else:
            out_ref[...] = (total[...] + part).astype(out_ref.dtype)


def feed_forward(keep, att, ups, downs):
    tokens = ROWS * COLS
    vmem = pl.BlockSpec(memory_space=pltpu.VMEM)
    hbm = pl.BlockSpec(memory_space=pl.ANY)
    return pl.pallas_call(
        lambda *refs: forward_kernel(keep, *refs),
        name="feed_forward_own" if keep else "feed_forward_partner",
        in_specs=[hbm] * 11,
        out_specs=vmem,
        out_shape=jax.ShapeDtypeStruct((tokens, D), F32 if keep else BF16),
        scratch_shapes=[
            pltpu.VMEM((FF // 2, D), BF16),
            pltpu.VMEM((FF // 2, D), BF16),
            pltpu.VMEM((tokens, D), F32),
            pltpu.VMEM((tokens, D), BF16),
            pltpu.SemaphoreType.DMA((41,)),
        ],
        compiler_params=pltpu.CompilerParams(vmem_limit_bytes=GRANT),
        cost_estimate=pl.CostEstimate(flops=2 * tokens * D * FF, bytes_accessed=6_000_000, transcendentals=tokens * FF // 2),
    )(att, *ups, *downs)


def swap(x, axis):
    return lax.ppermute(x, axis, [(0, 1), (1, 0)])


def ring_from_all(mine, axis):
    on = [(i, (i + 1) % 4) for i in range(4)]
    back = [(i, (i - 1) % 4) for i in range(4)]
    behind = lax.ppermute(mine, axis, on)
    ahead = lax.ppermute(mine, axis, back)
    half = mine.shape[1] // 2
    far_on = lax.ppermute(behind[:, :half], axis, on)
    return [mine, behind, ahead, far_on, lax.ppermute(ahead[:, half:], axis, back)]


def row_from_all(mine, axis):
    moves = (1, -1, 2)
    got = [lax.ppermute(mine, axis, [(i, (i + by) % 4) for i in range(4)]) for by in moves]
    return jnp.stack([mine, *got], axis=0)


def gathered_weights(expand, reduce):
    n = expand.shape[0]
    across = swap(jnp.concatenate([expand, reduce], axis=0), "mz")
    ups = row_from_all(jnp.concatenate([expand, across[:n]], axis=0), "mx")
    downs = row_from_all(jnp.concatenate([reduce, across[n:]], axis=0), "my")
    return ring_from_all(ups, "my"), ring_from_all(downs, "mx")


def strip_choice():
    lane = lax.optimization_barrier(jnp.arange(WIN * 15 * WIN))
    key_col = lane // (15 * WIN)
    block = lane // WIN % 15
    wanted = (14 - block) * 15 + key_col - lane % WIN + 7
    return jnp.where(jnp.arange(225)[:, None] == wanted[None, :], 1.0, 0.0).astype(F32)


def body(
    noisy_latents,
    frames,
    encoder_members,
    window_shift,
    encoder_in,
    encoder_out,
    joint_weight,
    query_weight,
    keyvalue_weight,
    output_weight,
    position_bias,
    expand_weight,
    reduce_weight,
):
    tokens = ROWS * COLS
    margin = WIN // 2
    bands = lax.axis_size("lat")
    member = lax.axis_index(MEMBER)
    core = lax.axis_index("core")
    is_second = member == encoder_members[1]
    is_source = jnp.logical_or(member == encoder_members[0], is_second)
    shift = window_shift[0]
    noisy = noisy_latents.reshape(tokens, D)
    down_pairs = [(i, i + 1) for i in range(bands - 1)]
    up_pairs = [(i + 1, i) for i in range(bands - 1)]
    edge = margin * COLS

    enc_scal = jnp.stack([is_source.astype(jnp.int32), 1 + is_second.astype(jnp.int32), core])
    keep, send = encode(enc_scal, frames.reshape(tokens, D), encoder_in, encoder_out, joint_weight)

    noisy_up = lax.ppermute(noisy[tokens - edge :], "lat", down_pairs)
    noisy_down = lax.ppermute(noisy[:edge], "lat", up_pairs)
    ups, downs = gathered_weights(expand_weight, reduce_weight)

    mine = (keep + swap(send, "core")).reshape(COLS // 2, ROWS, D)
    spread = lax.all_to_all(mine, PLANE, 0, 0, tiled=True)
    part = jnp.sum(spread.astype(F32), axis=0).astype(BF16)
    above = lax.ppermute(part[ROWS - margin :], "lat", down_pairs)
    below = lax.ppermute(part[:margin], "lat", up_pairs)
    part = jnp.concatenate([above, part, below], axis=0)
    part = part + swap(part, "mz")
    wide = jnp.broadcast_to(part[None], (COLS // 2, *part.shape))
    mine = lax.all_to_all(wide, PLANE, 0, 0, tiled=True)
    other = swap(mine, "core")

    noisy_wide = noisy_share(jnp.stack([shift, shift]), noisy_up, noisy, noisy_down, joint_weight)
    strip = jnp.dot(position_bias, strip_choice(), precision=lax.Precision.HIGHEST, preferred_element_type=F32)
    strip = strip.reshape(H, WIN, 15 * WIN)
    att_scal = jnp.stack([shift, core, lax.axis_index("lat"), jnp.int32(bands - 1)])
    attended = attend(att_scal, noisy_wide, mine, other, strip, query_weight, keyvalue_weight, output_weight)
    partner = swap(attended, "core")
    own = feed_forward(True, attended, ups, downs)
    theirs = feed_forward(False, partner, ups, downs)
    back = swap(theirs, "core")
    return (own + back.astype(F32)).astype(BF16).reshape(noisy_latents.shape)


def solution(mesh):
    finer = Mesh(mesh.devices.reshape(4, 4, 2, 2, mesh.shape["lat"]), (*MEMBER, "lat"))
    placed = (
        P(MEMBER, "lat", None, None),
        P(MEMBER, "lat", None, None),
        *([P()] * 9),
        P(MEMBER, None),
        P(MEMBER, None),
    )
    return jax.shard_map(
        body,
        mesh=finer,
        in_specs=placed,
        out_specs=P(MEMBER, "lat", None, None),
        check_vma=False,
    )
```

```python
import jax
import jax.numpy as jnp
from jax import lax
from jax.experimental import pallas as pl
from jax.experimental.pallas import tpu as pltpu
from jax.sharding import Mesh
from jax.sharding import PartitionSpec as P

HD = 64
WIN = 8
D = 768
H = 12
FF = 3072
ROWS = 16
COLS = 32
NLAT = 64
GROUPS = 3
MEMBER = ("mx", "my", "mz", "core")
PLANE = ("mx", "my")
EPS = 1e-06
F32 = jnp.float32
BF16 = jnp.bfloat16
axis_index = lax.axis_index


def in_hbm(x):
    return pltpu.with_memory_space_constraint(x, pltpu.HBM)


def dot(a, b):
    return jnp.dot(a, b, preferred_element_type=F32)


def dot_nt(a, b):
    return lax.dot_general(a, b, (((1,), (1,)), ((), ())), preferred_element_type=F32)


def dot_tn(a, b):
    return lax.dot_general(a, b, (((0,), (0,)), ((), ())), preferred_element_type=F32)


def normalised(x):
    scale = lax.rsqrt(jnp.mean(x * x, axis=-1, keepdims=True) + EPS)
    return (x * scale).astype(BF16)


def one_hot(wanted, width):
    lanes = lax.broadcasted_iota(jnp.int32, (wanted.shape[0], width), 1)
    return jnp.where(lanes == wanted, 1.0, 0.0).astype(BF16)


def row_ids(count):
    return lax.broadcasted_iota(jnp.int32, (count, 1), 0)


def window_place(count, shift):
    t = row_ids(count)
    row = (t // WIN) % WIN
    col = ((t // (WIN * WIN)) * WIN + t % WIN - shift + COLS) % COLS
    return row, col


def encode_kernel(chosen, frame_hbm, in_hbm, out_hbm, joint_hbm, keep_ref, send_ref, frame, w_in, w_out, w_slot, sems):
    own_core = axis_index("core")
    member = axis_index(MEMBER)
    is_second = member == chosen[1]
    is_source = jnp.logical_or(member == chosen[0], is_second)
    slot = jnp.where(is_second, 2, 1)
    copies = [
        pltpu.make_async_copy(frame_hbm, frame, sems.at[0]),
        pltpu.make_async_copy(in_hbm, w_in, sems.at[1]),
        pltpu.make_async_copy(out_hbm, w_out, sems.at[2]),
        pltpu.make_async_copy(joint_hbm.at[pl.ds(pl.multiple_of(slot * D, D), D), :], w_slot, sems.at[3]),
    ]
    for c in copies:
        c.start()
    tokens = ROWS * COLS
    t = row_ids(tokens)
    half = tokens // 2
    core = jnp.where(t < half, own_core, 1 - own_core)
    col = core * (COLS // 2) + (t % half) // ROWS
    order = one_hot((t % ROWS) * COLS + col, tokens)
    copies[0].wait()
    ordered = dot(order, frame[...]).astype(BF16)
    copies[1].wait()
    hidden = jax.nn.gelu(dot(ordered, w_in[...])).astype(BF16)
    copies[2].wait()
    condition = dot(hidden, w_out[...]).astype(BF16)
    copies[3].wait()
    term = dot(condition, w_slot[...])
    term = jnp.where(is_source, term, 0.0).astype(BF16)
    keep_ref[...] = term[:half]
    send_ref[...] = term[half:]


def encode(chosen, frame, w_in, w_out, joint):
    tokens = ROWS * COLS
    any_spec = pl.BlockSpec(memory_space=pltpu.HBM)
    out = jax.ShapeDtypeStruct((tokens // 2, D), BF16)
    return pl.pallas_call(
        encode_kernel,
        name="encode",
        in_specs=[pl.BlockSpec(memory_space=pltpu.SMEM)] + [any_spec] * 4,
        out_shape=(out, out),
        scratch_shapes=[
            pltpu.VMEM((tokens, D), BF16),
            pltpu.VMEM((D, D), BF16),
            pltpu.VMEM((D, D), BF16),
            pltpu.VMEM((D, D), BF16),
            pltpu.SemaphoreType.DMA((4,)),
        ],
        compiler_params=pltpu.CompilerParams(vmem_limit_bytes=24 << 20),
        cost_estimate=pl.CostEstimate(flops=2 * tokens * D * (3 * D + tokens), bytes_accessed=6_000_000, transcendentals=tokens * D),
    )(chosen, *map(in_hbm, (frame, w_in, w_out, joint)))


def attend_kernel(shift_ref, up_ref, own_ref, down_ref, mine_ref, other_ref, strip_ref, w0_hbm, wq_hbm, wkv_hbm, wo_hbm, out_ref, bias_ref, stream_ref, normed_ref, qkv_ref, mixed_ref, w0, wqkv, wo, sems):
    copies = [
        pltpu.make_async_copy(w0_hbm.at[pl.ds(0, D), :], w0, sems.at[0]),
        pltpu.make_async_copy(wq_hbm, wqkv.at[:, :D], sems.at[1]),
        pltpu.make_async_copy(wkv_hbm, wqkv.at[:, D:], sems.at[2]),
        pltpu.make_async_copy(wo_hbm, wo, sems.at[3]),
    ]
    for c in copies:
        c.start()
    shift = shift_ref[0]
    core = axis_index("core")
    band = axis_index("lat")
    last = NLAT // ROWS - 1
    pairs = H // 2
    for h in range(H):
        for r in range(WIN):
            at = WIN * (WIN - 1 - r)
            bias_ref[h // 2, WIN * r : WIN * (r + 1), (h % 2) * HD : (h % 2 + 1) * HD] = strip_ref[h, :, at : at + HD]
    row, col = window_place(256, shift)
    half = COLS // 2
    place = (col % half) * WIN + row
    from_mine = one_hot(jnp.where(col // half == core, place, -1), 128)
    from_other = one_hot(jnp.where(col // half == core, -1, place), 128)
    order = one_hot(row * COLS + col, 256)
    tokens = ((up_ref[...], own_ref[:128, :]), (own_ref[128:384, :],), (own_ref[384:, :], down_ref[...]))
    for g in range(GROUPS):
        placed = dot(order, jnp.concatenate(tokens[g], axis=0) if len(tokens[g]) > 1 else tokens[g][0])
        mixed_ref[g * 256 : (g + 1) * 256, :] = placed.astype(BF16)
    copies[0].wait()
    noisy = dot(mixed_ref[...], w0[...])
    for g in range(GROUPS):
        mine = mine_ref[:, g * WIN : (g + 1) * WIN, :].astype(F32).reshape(128, D).astype(BF16)
        other = other_ref[:, g * WIN : (g + 1) * WIN, :].astype(F32).reshape(128, D).astype(BF16)
        stream = (noisy[g * 256 : (g + 1) * 256] + (dot(from_mine, mine) + dot(from_other, other))).astype(BF16)
        stream_ref[g * 256 : (g + 1) * 256, :] = stream
        normed_ref[g * 256 : (g + 1) * 256, :] = normalised(stream.astype(F32))
    copies[1].wait()
    copies[2].wait()
    for n in range(3):
        cols = slice(n * D, (n + 1) * D)
        qkv_ref[:, cols] = dot(normed_ref[...], wqkv[:, cols]).astype(BF16)
    low = lax.broadcasted_iota(jnp.int32, (64, 128), 1) < HD
    key_row = lax.broadcasted_iota(jnp.int32, (64, 128), 0)

    def window(w, carry):
        rows = pl.ds(pl.multiple_of(w * 64, 64), 64)
        hide_top = jnp.logical_and(w < 4, band == 0)
        hide_end = jnp.logical_and(w >= 8, band == last)
        first = jnp.where(hide_top, 32, 0)
        end = jnp.where(hide_end, 32, 64)
        seen = jnp.logical_and(key_row >= first, key_row < end)
        scores = []
        for p in range(pairs):
            q = qkv_ref[rows, p * 128 : (p + 1) * 128]
            k = qkv_ref[rows, D + p * 128 : D + (p + 1) * 128]
            zero = jnp.zeros_like(q)
            both = jnp.concatenate([jnp.where(low, q, zero), jnp.where(low, zero, q)], axis=0)
            scores.append(dot_nt(k, both))
        scores = [jnp.where(seen, s * HD ** (-0.5) + bias_ref[p], -1e30) for p, s in enumerate(scores)]
        tops = [jnp.max(s, axis=0, keepdims=True) for s in scores]
        weights = [jnp.exp(s - m) for s, m in zip(scores, tops)]
        sums = [1.0 / jnp.sum(e, axis=0, keepdims=True) for e in weights]
        probs = [(e * i).astype(BF16) for e, i in zip(weights, sums)]
        got = [dot_tn(probs[p], qkv_ref[rows, 2 * D + p * 128 : 2 * D + (p + 1) * 128]) for p in range(pairs)]
        for p in range(pairs):
            mixed_ref[rows, p * 128 : (p + 1) * 128] = jnp.where(low, got[p][:64], got[p][64:]).astype(BF16)
        return carry

    lax.fori_loop(0, 4 * GROUPS, window, 0, unroll=2)
    t = row_ids(128)
    moved = (t % COLS + shift) % COLS
    base = (moved // WIN) * 64 + (t // COLS) * WIN + moved % WIN
    for b in range(4):
        g, first = divmod(4 * b + 4, WIN)
        back = one_hot(base + first * WIN, 256)
        mixed = dot(back, mixed_ref[g * 256 : (g + 1) * 256, :]).astype(BF16)
        normed_ref[b * 128 : (b + 1) * 128, :] = mixed
        qkv_ref[b * 128 : (b + 1) * 128, :D] = dot(back, stream_ref[g * 256 : (g + 1) * 256, :]).astype(BF16)
    copies[3].wait()
    tokens = ROWS * COLS
    out_ref[...] = (qkv_ref[:tokens, :D].astype(F32) + dot(normed_ref[:tokens, :], wo[...])).astype(BF16)


def attend(shift, up, own, down, mine, other, strip, joint, wq, wkv, wo):
    args = (up, own, down, mine, other, strip)
    return pl.pallas_call(
        attend_kernel,
        name="attend",
        in_specs=[
            pl.BlockSpec(memory_space=pltpu.SMEM),
            *(pl.BlockSpec(memory_space=pltpu.VMEM) for _ in args),
            *(pl.BlockSpec(memory_space=pltpu.HBM) for _ in range(4)),
        ],
        out_specs=pl.BlockSpec(memory_space=pltpu.VMEM),
        out_shape=jax.ShapeDtypeStruct((ROWS * COLS, D), BF16),
        scratch_shapes=[
            pltpu.VMEM((H // 2, 64, 128), F32),
            pltpu.VMEM((768, D), BF16),
            pltpu.VMEM((768, D), BF16),
            pltpu.VMEM((768, 3 * D), BF16),
            pltpu.VMEM((768, D), BF16),
            pltpu.VMEM((D, D), BF16),
            pltpu.VMEM((D, 3 * D), BF16),
            pltpu.VMEM((D, D), BF16),
            pltpu.SemaphoreType.DMA((4,)),
        ],
        compiler_params=pltpu.CompilerParams(vmem_limit_bytes=36 << 20),
        cost_estimate=pl.CostEstimate(flops=2 * 768 * D * 6 * D, bytes_accessed=10_000_000, transcendentals=768 * 64 * 12),
    )(shift, *args, *map(in_hbm, (joint, wq, wkv, wo)))


def forward_kernel(keep, att_ref, *refs):
    ups = refs[0:4]
    downs = refs[4:8]
    out_ref, total = refs[8:]
    unit = ups[0].shape[1]
    x = att_ref[...].astype(F32)
    second = normalised(x)
    for n in range(2):
        rings = (2 * n, 2 * n + 1)
        up = jnp.concatenate([ups[i][...].reshape(4 * unit, D) for i in rings], axis=0)
        hidden = jax.nn.gelu(dot_nt(second, up)).astype(BF16)
        down = jnp.concatenate([downs[j][i] for i in rings for j in range(4)], axis=0)
        part = dot(hidden, down)
        if n == 0:
            total[...] = x + part if keep else part
        else:
            out_ref[...] = (total[...] + part).astype(out_ref.dtype)


def feed_forward(keep, att, ups, downs):
    tokens = ROWS * COLS
    vmem = pl.BlockSpec(memory_space=pltpu.VMEM)
    return pl.pallas_call(
        lambda *refs: forward_kernel(keep, *refs),
        name="feed_forward_own" if keep else "feed_forward_partner",
        in_specs=[vmem] * 9,
        out_specs=vmem,
        out_shape=jax.ShapeDtypeStruct((tokens, D), F32 if keep else BF16),
        scratch_shapes=[pltpu.VMEM((tokens, D), F32)],
        compiler_params=pltpu.CompilerParams(vmem_limit_bytes=20 << 20),
        cost_estimate=pl.CostEstimate(flops=2 * tokens * D * FF, bytes_accessed=6_000_000, transcendentals=tokens * FF // 2),
    )(att, *ups, *downs)


def swap(x, axis):
    return lax.ppermute(x, axis, [(0, 1), (1, 0)])


def ring_from_all(mine, axis):
    on = [(i, (i + 1) % 4) for i in range(4)]
    back = [(i, (i - 1) % 4) for i in range(4)]
    behind = lax.ppermute(mine, axis, on)
    ahead = lax.ppermute(mine, axis, back)
    return [mine, behind, ahead, lax.ppermute(behind, axis, on)]


def row_from_all(mine, axis):
    moves = (1, -1, 2)
    got = [lax.ppermute(mine, axis, [(i, (i + by) % 4) for i in range(4)]) for by in moves]
    return jnp.stack([mine, *got], axis=0)


def gathered_weights(expand, reduce):
    n = expand.shape[0]
    across = swap(jnp.concatenate([expand, reduce], axis=0), "mz")
    ups = row_from_all(jnp.concatenate([expand, across[:n]], axis=0), "mx")
    downs = row_from_all(jnp.concatenate([reduce, across[n:]], axis=0), "my")
    return ring_from_all(ups, "my"), ring_from_all(downs, "mx")


def strip_choice():
    lane = lax.optimization_barrier(jnp.arange(WIN * 15 * WIN))
    key_col = lane // (15 * WIN)
    block = lane // WIN % 15
    wanted = (14 - block) * 15 + key_col - lane % WIN + 7
    return jnp.where(jnp.arange(225)[:, None] == wanted[None, :], 1.0, 0.0).astype(F32)


def body(
    noisy_latents,
    frames,
    encoder_members,
    window_shift,
    encoder_in,
    encoder_out,
    joint_weight,
    query_weight,
    keyvalue_weight,
    output_weight,
    position_bias,
    expand_weight,
    reduce_weight,
):
    tokens = ROWS * COLS
    margin = WIN // 2
    bands = lax.axis_size("lat")
    noisy = noisy_latents.reshape(tokens, D)
    to_next = [(i, (i + 1) % bands) for i in range(bands)]
    to_last = [(i, (i - 1) % bands) for i in range(bands)]
    edge = margin * COLS

    keep, send = encode(encoder_members, frames.reshape(tokens, D), encoder_in, encoder_out, joint_weight)
    ups, downs = gathered_weights(expand_weight, reduce_weight)
    noisy_up = lax.ppermute(noisy[tokens - edge :], "lat", to_next)
    noisy_down = lax.ppermute(noisy[:edge], "lat", to_last)

    mine = (keep + swap(send, "core")).reshape(COLS // 2, ROWS, D)
    spread = lax.all_to_all(mine, PLANE, 0, 0, tiled=True)
    part = jnp.sum(spread.astype(F32), axis=0).astype(BF16)
    above = lax.ppermute(part[ROWS - margin :], "lat", to_next)
    below = lax.ppermute(part[:margin], "lat", to_last)
    part = jnp.concatenate([above, part, below], axis=0)
    part = part + swap(part, "mz")
    wide = jnp.broadcast_to(part[None], (COLS // 2, *part.shape))
    mine = lax.all_to_all(wide, PLANE, 0, 0, tiled=True)
    other = swap(mine, "core")

    strip = jnp.dot(position_bias, strip_choice(), precision=lax.Precision.HIGHEST, preferred_element_type=F32)
    strip = strip.reshape(H, WIN, 15 * WIN)
    attended = attend(
        window_shift, noisy_up, noisy, noisy_down, mine, other, strip, joint_weight, query_weight, keyvalue_weight, output_weight
    )
    partner = swap(attended, "core")
    own = feed_forward(True, attended, ups, downs)
    theirs = feed_forward(False, partner, ups, downs)
    back = swap(theirs, "core")
    return (own + back.astype(F32)).astype(BF16).reshape(noisy_latents.shape)


def solution(mesh):
    finer = Mesh(mesh.devices.reshape(4, 4, 2, 2, mesh.shape["lat"]), (*MEMBER, "lat"))
    placed = (
        P(MEMBER, "lat", None, None),
        P(MEMBER, "lat", None, None),
        *([P()] * 9),
        P(MEMBER, None),
        P(MEMBER, None),
    )
    return jax.shard_map(
        body,
        mesh=finer,
        in_specs=placed,
        out_specs=P(MEMBER, "lat", None, None),
        check_vma=False,
    )
```

```python
import jax
import jax.numpy as jnp
from jax import lax
from jax.experimental import pallas as pl
from jax.experimental.pallas import tpu as pltpu
from jax.sharding import Mesh
from jax.sharding import PartitionSpec as P

HD = 64
WIN = 8
D = 768
H = 12
FF = 3072
ROWS = 16
COLS = 32
NLAT = 64
EDGE = WIN // 2 * COLS
GROUPS = 3
MEMBER = ("mx", "my", "mz", "core")
PLANE = ("mx", "my")
EPS = 1e-06
F32 = jnp.float32
BF16 = jnp.bfloat16
axis_index = lax.axis_index


def in_hbm(x):
    return pltpu.with_memory_space_constraint(x, pltpu.HBM)


def dot(a, b):
    return jnp.dot(a, b, preferred_element_type=F32)


def dot_nt(a, b):
    return lax.dot_general(a, b, (((1,), (1,)), ((), ())), preferred_element_type=F32)


def dot_tn(a, b):
    return lax.dot_general(a, b, (((0,), (0,)), ((), ())), preferred_element_type=F32)


def normalised(x):
    scale = lax.rsqrt(jnp.mean(x * x, axis=-1, keepdims=True) + EPS)
    return (x * scale).astype(BF16)


def one_hot(wanted, width):
    lanes = lax.broadcasted_iota(jnp.int32, (wanted.shape[0], width), 1)
    return jnp.where(lanes == wanted, 1.0, 0.0).astype(BF16)


def row_ids(count):
    return lax.broadcasted_iota(jnp.int32, (count, 1), 0)


def window_place(count, shift):
    t = row_ids(count)
    row = (t // WIN) % WIN
    col = ((t // (WIN * WIN)) * WIN + t % WIN - shift + COLS) % COLS
    return row, col


def encode_kernel(chosen, frame_hbm, in_hbm, out_hbm, joint_hbm, noisy_hbm, keep_ref, send_ref, head_ref, tail_ref, frame, w_in, w_out, w_slot, sems):
    own_core = axis_index("core")
    member = axis_index(MEMBER)
    is_second = member == chosen[1]
    is_source = jnp.logical_or(member == chosen[0], is_second)
    slot = jnp.where(is_second, 2, 1)
    copies = [
        pltpu.make_async_copy(frame_hbm, frame, sems.at[0]),
        pltpu.make_async_copy(in_hbm, w_in, sems.at[1]),
        pltpu.make_async_copy(out_hbm, w_out, sems.at[2]),
        pltpu.make_async_copy(joint_hbm.at[pl.ds(pl.multiple_of(slot * D, D), D), :], w_slot, sems.at[3]),
        pltpu.make_async_copy(noisy_hbm.at[pl.ds(0, EDGE), :], head_ref, sems.at[4]),
        pltpu.make_async_copy(noisy_hbm.at[pl.ds(ROWS * COLS - EDGE, EDGE), :], tail_ref, sems.at[5]),
    ]
    for c in copies:
        c.start()
    tokens = ROWS * COLS
    t = row_ids(tokens)
    half = tokens // 2
    core = jnp.where(t < half, own_core, 1 - own_core)
    col = core * (COLS // 2) + (t % half) // ROWS
    order = one_hot((t % ROWS) * COLS + col, tokens)
    copies[0].wait()
    ordered = dot(order, frame[...]).astype(BF16)
    copies[1].wait()
    hidden = jax.nn.gelu(dot(ordered, w_in[...])).astype(BF16)
    copies[2].wait()
    condition = dot(hidden, w_out[...]).astype(BF16)
    copies[3].wait()
    term = dot(condition, w_slot[...])
    term = jnp.where(is_source, term, 0.0).astype(BF16)
    keep_ref[...] = term[:half]
    send_ref[...] = term[half:]
    copies[4].wait()
    copies[5].wait()


def encode(chosen, frame, w_in, w_out, joint, noisy):
    tokens = ROWS * COLS
    any_spec = pl.BlockSpec(memory_space=pltpu.HBM)
    out = jax.ShapeDtypeStruct((tokens // 2, D), BF16)
    rim = jax.ShapeDtypeStruct((EDGE, D), BF16)
    return pl.pallas_call(
        encode_kernel,
        name="encode",
        in_specs=[pl.BlockSpec(memory_space=pltpu.SMEM)] + [any_spec] * 5,
        out_shape=(out, out, rim, rim),
        scratch_shapes=[
            pltpu.VMEM((tokens, D), BF16),
            pltpu.VMEM((D, D), BF16),
            pltpu.VMEM((D, D), BF16),
            pltpu.VMEM((D, D), BF16),
            pltpu.SemaphoreType.DMA((6,)),
        ],
        compiler_params=pltpu.CompilerParams(vmem_limit_bytes=24 << 20),
        cost_estimate=pl.CostEstimate(flops=2 * tokens * D * (3 * D + tokens), bytes_accessed=6_000_000, transcendentals=tokens * D),
    )(chosen, *map(in_hbm, (frame, w_in, w_out, joint, noisy)))


def attend_kernel(shift_ref, up_ref, own_ref, down_ref, mine_ref, other_ref, strip_ref, w0_hbm, wq_hbm, wkv_hbm, wo_hbm, out_ref, bias_ref, stream_ref, normed_ref, qkv_ref, mixed_ref, w0, wqkv, wo, sems):
    copies = [
        pltpu.make_async_copy(w0_hbm.at[pl.ds(0, D), :], w0, sems.at[0]),
        pltpu.make_async_copy(wq_hbm, wqkv.at[:, :D], sems.at[1]),
        pltpu.make_async_copy(wkv_hbm, wqkv.at[:, D:], sems.at[2]),
        pltpu.make_async_copy(wo_hbm, wo, sems.at[3]),
    ]
    for c in copies:
        c.start()
    shift = shift_ref[0]
    core = axis_index("core")
    band = axis_index("lat")
    last = NLAT // ROWS - 1
    pairs = H // 2
    for h in range(H):
        for r in range(WIN):
            at = WIN * (WIN - 1 - r)
            bias_ref[h // 2, WIN * r : WIN * (r + 1), (h % 2) * HD : (h % 2 + 1) * HD] = strip_ref[h, :, at : at + HD]
    row, col = window_place(256, shift)
    half = COLS // 2
    place = (col % half) * WIN + row
    placing = one_hot(jnp.where(col // half == core, place, place + 128), 256)
    order = one_hot(row * COLS + col, 256)
    tokens = ((up_ref[...], own_ref[:128, :]), (own_ref[128:384, :],), (own_ref[384:, :], down_ref[...]))
    for g in range(GROUPS):
        placed = dot(order, jnp.concatenate(tokens[g], axis=0) if len(tokens[g]) > 1 else tokens[g][0])
        mixed_ref[g * 256 : (g + 1) * 256, :] = placed.astype(BF16)
    copies[0].wait()
    noisy = dot(mixed_ref[...], w0[...])
    for g in range(GROUPS):
        both = [half_ref[:, g * WIN : (g + 1) * WIN, :].astype(F32).reshape(128, D) for half_ref in (mine_ref, other_ref)]
        condition = jnp.concatenate(both, axis=0).astype(BF16)
        stream = (noisy[g * 256 : (g + 1) * 256] + dot(placing, condition)).astype(BF16)
        stream_ref[g * 256 : (g + 1) * 256, :] = stream
        normed_ref[g * 256 : (g + 1) * 256, :] = normalised(stream.astype(F32))
    copies[1].wait()
    copies[2].wait()
    for n in range(3):
        cols = slice(n * D, (n + 1) * D)
        made = dot(normed_ref[...], wqkv[:, cols])
        qkv_ref[:, cols] = (made * HD ** (-0.5) if n == 0 else made).astype(BF16)
    low = lax.broadcasted_iota(jnp.int32, (64, 128), 1) < HD
    key_row = lax.broadcasted_iota(jnp.int32, (64, 128), 0)

    def window(w, carry):
        rows = pl.ds(pl.multiple_of(w * 64, 64), 64)
        hide_top = jnp.logical_and(w < 4, band == 0)
        hide_end = jnp.logical_and(w >= 8, band == last)
        first = jnp.where(hide_top, 32, 0)
        end = jnp.where(hide_end, 32, 64)
        seen = jnp.logical_and(key_row >= first, key_row < end)
        scores = []
        for p in range(pairs):
            q = qkv_ref[rows, p * 128 : (p + 1) * 128]
            k = qkv_ref[rows, D + p * 128 : D + (p + 1) * 128]
            zero = jnp.zeros_like(q)
            both = jnp.concatenate([jnp.where(low, q, zero), jnp.where(low, zero, q)], axis=0)
            scores.append(dot_nt(k, both))
        scores = [jnp.where(seen, s + bias_ref[p], -1e30) for p, s in enumerate(scores)]
        tops = [jnp.max(s, axis=0, keepdims=True) for s in scores]
        weights = [jnp.exp(s - m) for s, m in zip(scores, tops)]
        sums = [1.0 / jnp.sum(e, axis=0, keepdims=True) for e in weights]
        probs = [(e * i).astype(BF16) for e, i in zip(weights, sums)]
        got = [dot_tn(probs[p], qkv_ref[rows, 2 * D + p * 128 : 2 * D + (p + 1) * 128]) for p in range(pairs)]
        for p in range(pairs):
            mixed_ref[rows, p * 128 : (p + 1) * 128] = jnp.where(low, got[p][:64], got[p][64:]).astype(BF16)
        return carry

    lax.fori_loop(0, 4 * GROUPS, window, 0, unroll=2)
    t = row_ids(128)
    moved = (t % COLS + shift) % COLS
    base = (moved // WIN) * 64 + (t // COLS) * WIN + moved % WIN
    for b in range(4):
        g, first = divmod(4 * b + 4, WIN)
        back = one_hot(base + first * WIN, 256)
        mixed = dot(back, mixed_ref[g * 256 : (g + 1) * 256, :]).astype(BF16)
        normed_ref[b * 128 : (b + 1) * 128, :] = mixed
        qkv_ref[b * 128 : (b + 1) * 128, :D] = dot(back, stream_ref[g * 256 : (g + 1) * 256, :]).astype(BF16)
    copies[3].wait()
    tokens = ROWS * COLS
    out_ref[...] = (qkv_ref[:tokens, :D].astype(F32) + dot(normed_ref[:tokens, :], wo[...])).astype(BF16)


def attend(shift, up, own, down, mine, other, strip, joint, wq, wkv, wo):
    args = (up, own, down, mine, other, strip)
    return pl.pallas_call(
        attend_kernel,
        name="attend",
        in_specs=[
            pl.BlockSpec(memory_space=pltpu.SMEM),
            *(pl.BlockSpec(memory_space=pltpu.VMEM) for _ in args),
            *(pl.BlockSpec(memory_space=pltpu.HBM) for _ in range(4)),
        ],
        out_specs=pl.BlockSpec(memory_space=pltpu.VMEM),
        out_shape=jax.ShapeDtypeStruct((ROWS * COLS, D), BF16),
        scratch_shapes=[
            pltpu.VMEM((H // 2, 64, 128), F32),
            pltpu.VMEM((768, D), BF16),
            pltpu.VMEM((768, D), BF16),
            pltpu.VMEM((768, 3 * D), BF16),
            pltpu.VMEM((768, D), BF16),
            pltpu.VMEM((D, D), BF16),
            pltpu.VMEM((D, 3 * D), BF16),
            pltpu.VMEM((D, D), BF16),
            pltpu.SemaphoreType.DMA((4,)),
        ],
        compiler_params=pltpu.CompilerParams(vmem_limit_bytes=36 << 20),
        cost_estimate=pl.CostEstimate(flops=2 * 768 * D * 6 * D, bytes_accessed=10_000_000, transcendentals=768 * 64 * 12),
    )(shift, *args, *map(in_hbm, (joint, wq, wkv, wo)))


def forward_kernel(keep, att_ref, *refs):
    ups = refs[0:4]
    downs = refs[4:8]
    out_ref, total = refs[8:]
    unit = ups[0].shape[1]
    x = att_ref[...].astype(F32)
    second = normalised(x)
    for n in range(2):
        rings = (2 * n, 2 * n + 1)
        up = jnp.concatenate([ups[i][...].reshape(4 * unit, D) for i in rings], axis=0)
        hidden = jax.nn.gelu(dot_nt(second, up)).astype(BF16)
        down = jnp.concatenate([downs[j][i] for i in rings for j in range(4)], axis=0)
        part = dot(hidden, down)
        if n == 0:
            total[...] = x + part if keep else part
        else:
            out_ref[...] = (total[...] + part).astype(out_ref.dtype)


def feed_forward(keep, att, ups, downs):
    tokens = ROWS * COLS
    vmem = pl.BlockSpec(memory_space=pltpu.VMEM)
    return pl.pallas_call(
        lambda *refs: forward_kernel(keep, *refs),
        name="feed_forward_own" if keep else "feed_forward_partner",
        in_specs=[vmem] * 9,
        out_specs=vmem,
        out_shape=jax.ShapeDtypeStruct((tokens, D), F32 if keep else BF16),
        scratch_shapes=[pltpu.VMEM((tokens, D), F32)],
        compiler_params=pltpu.CompilerParams(vmem_limit_bytes=20 << 20),
        cost_estimate=pl.CostEstimate(flops=2 * tokens * D * FF, bytes_accessed=6_000_000, transcendentals=tokens * FF // 2),
    )(att, *ups, *downs)


def swap(x, axis):
    return lax.ppermute(x, axis, [(0, 1), (1, 0)])


def ring_from_all(mine, axis):
    on = [(i, (i + 1) % 4) for i in range(4)]
    back = [(i, (i - 1) % 4) for i in range(4)]
    behind = lax.ppermute(mine, axis, on)
    ahead = lax.ppermute(mine, axis, back)
    return [mine, behind, ahead, lax.ppermute(behind, axis, on)]


PAIRS = {"a": [(0, 1), (1, 0), (2, 3), (3, 2)], "b": [(1, 2), (2, 1), (3, 0), (0, 3)]}


def held_back(x, after):
    first = lax.slice(after, (0,) * after.ndim, (1,) * after.ndim).reshape((1,) * x.ndim)
    return jnp.where(first < jnp.inf, x, jnp.zeros_like(x))


def row_start(mine, axis):
    return mine, lax.ppermute(mine, axis, PAIRS["a"])


def row_rest(mine, first, after, axis):
    pair = jnp.stack([mine, held_back(first, after)], axis=0)
    return mine, first, lax.ppermute(pair, axis, PAIRS["b"])


def row_sorted(mine, first, second, after, axis):
    even = lax.axis_index(axis) % 2 == 0
    second = held_back(second, after)
    behind = jnp.where(even, second[0], first)
    return jnp.stack([mine, behind, jnp.where(even, first, second[0]), second[1]], axis=0)


def weights_start(expand, reduce):
    n = expand.shape[0]
    across = swap(jnp.concatenate([expand, reduce], axis=0), "mz")
    ups = row_start(jnp.concatenate([expand, across[:n]], axis=0), "mx")
    return ups, row_start(jnp.concatenate([reduce, across[n:]], axis=0), "my")


def strip_choice():
    lane = lax.optimization_barrier(jnp.arange(WIN * 15 * WIN))
    key_col = lane // (15 * WIN)
    block = lane // WIN % 15
    wanted = (14 - block) * 15 + key_col - lane % WIN + 7
    return jnp.where(jnp.arange(225)[:, None] == wanted[None, :], 1.0, 0.0).astype(F32)


def body(
    noisy_latents,
    frames,
    encoder_members,
    window_shift,
    encoder_in,
    encoder_out,
    joint_weight,
    query_weight,
    keyvalue_weight,
    output_weight,
    position_bias,
    expand_weight,
    reduce_weight,
):
    tokens = ROWS * COLS
    margin = WIN // 2
    bands = lax.axis_size("lat")
    noisy = noisy_latents.reshape(tokens, D)
    to_next = [(i, (i + 1) % bands) for i in range(bands)]
    to_last = [(i, (i - 1) % bands) for i in range(bands)]

    keep, send, head, tail = encode(
        encoder_members, frames.reshape(tokens, D), encoder_in, encoder_out, joint_weight, noisy
    )
    ups, downs = weights_start(expand_weight, reduce_weight)
    noisy_up = lax.ppermute(tail, "lat", to_next)
    noisy_down = lax.ppermute(head, "lat", to_last)

    handed = swap(send, "core")
    mine = (keep + handed).reshape(COLS // 2, ROWS, D)
    spread = lax.all_to_all(mine, PLANE, 0, 0, tiled=True)
    ups = row_rest(*ups, handed, "mx")
    downs = row_rest(*downs, handed, "my")
    part = jnp.sum(spread.astype(F32), axis=0).astype(BF16)
    above = lax.ppermute(part[ROWS - margin :], "lat", to_next)
    below = lax.ppermute(part[:margin], "lat", to_last)
    ups = ring_from_all(row_sorted(*ups, above, "mx"), "my")
    downs = ring_from_all(row_sorted(*downs, above, "my"), "mx")
    part = jnp.concatenate([above, part, below], axis=0)
    part = part + swap(part, "mz")
    wide = jnp.broadcast_to(part[None], (COLS // 2, *part.shape))
    mine = lax.all_to_all(wide, PLANE, 0, 0, tiled=True)
    other = swap(mine, "core")

    strip = jnp.dot(position_bias, strip_choice(), precision=lax.Precision.HIGHEST, preferred_element_type=F32)
    strip = strip.reshape(H, WIN, 15 * WIN)
    attended = attend(
        window_shift, noisy_up, noisy, noisy_down, mine, other, strip, joint_weight, query_weight, keyvalue_weight, output_weight
    )
    partner = swap(attended, "core")
    own = feed_forward(True, attended, ups, downs)
    theirs = feed_forward(False, partner, ups, downs)
    back = swap(theirs, "core")
    return (own + back.astype(F32)).astype(BF16).reshape(noisy_latents.shape)


def solution(mesh):
    finer = Mesh(mesh.devices.reshape(4, 4, 2, 2, mesh.shape["lat"]), (*MEMBER, "lat"))
    placed = (
        P(MEMBER, "lat", None, None),
        P(MEMBER, "lat", None, None),
        *([P()] * 9),
        P(MEMBER, None),
        P(MEMBER, None),
    )
    return jax.shard_map(
        body,
        mesh=finer,
        in_specs=placed,
        out_specs=P(MEMBER, "lat", None, None),
        check_vma=False,
    )
```

```python
import jax
import jax.numpy as jnp
from jax import lax
from jax.experimental import pallas as pl
from jax.experimental.pallas import tpu as pltpu
from jax.sharding import Mesh
from jax.sharding import PartitionSpec as P

HD = 64
WIN = 8
D = 768
H = 12
FF = 3072
ROWS = 16
COLS = 32
NLAT = 64
EDGE = WIN // 2 * COLS
GROUPS = 3
MEMBER = ("mx", "my", "mz", "core")
PLANE = ("mx", "my")
EPS = 1e-06
F32 = jnp.float32
BF16 = jnp.bfloat16
axis_index = lax.axis_index


def in_hbm(x):
    return pltpu.with_memory_space_constraint(x, pltpu.HBM)


def dot(a, b):
    return jnp.dot(a, b, preferred_element_type=F32)


def dot_nt(a, b):
    return lax.dot_general(a, b, (((1,), (1,)), ((), ())), preferred_element_type=F32)


def dot_tn(a, b):
    return lax.dot_general(a, b, (((0,), (0,)), ((), ())), preferred_element_type=F32)


def normalised(x):
    scale = lax.rsqrt(jnp.mean(x * x, axis=-1, keepdims=True) + EPS)
    return (x * scale).astype(BF16)


def one_hot(wanted, width):
    lanes = lax.broadcasted_iota(jnp.int32, (wanted.shape[0], width), 1)
    return jnp.where(lanes == wanted, 1.0, 0.0).astype(BF16)


def row_ids(count):
    return lax.broadcasted_iota(jnp.int32, (count, 1), 0)


def window_place(count, shift):
    t = row_ids(count)
    row = (t // WIN) % WIN
    col = ((t // (WIN * WIN)) * WIN + t % WIN - shift + COLS) % COLS
    return row, col


def encode_kernel(chosen, frame_hbm, in_hbm, out_hbm, joint_hbm, keep_ref, send_ref, frame, w_in, w_out, w_slot, term_ref, sems):
    own_core = axis_index("core")
    member = axis_index(MEMBER)
    is_second = member == chosen[1]
    is_source = jnp.logical_or(member == chosen[0], is_second)
    slot = jnp.where(is_second, 2, 1)
    copies = [
        pltpu.make_async_copy(frame_hbm, frame, sems.at[0]),
        pltpu.make_async_copy(in_hbm, w_in, sems.at[1]),
        pltpu.make_async_copy(out_hbm, w_out, sems.at[2]),
        pltpu.make_async_copy(joint_hbm.at[pl.ds(pl.multiple_of(slot * D, D), D), :], w_slot, sems.at[3]),
    ]
    for c in copies:
        c.start()
    copies[0].wait()
    copies[1].wait()
    hidden = jax.nn.gelu(dot(frame[...], w_in[...])).astype(BF16)
    copies[2].wait()
    condition = dot(hidden, w_out[...]).astype(BF16)
    copies[3].wait()
    term = dot(condition, w_slot[...])
    term_ref[...] = jnp.where(is_source, term, 0.0)
    for half, out_ref in ((own_core, keep_ref), (1 - own_core, send_ref)):
        for slot, start in enumerate((jnp.where(half == 0, 0, 384), jnp.where(half == 0, 128, 256))):
            block = term_ref[pl.ds(pl.multiple_of(start, 128), 128), :]
            out_ref[:, slot * 8 : slot * 8 + 8, :] = block.reshape(16, 8, D).astype(BF16)


def encode(chosen, frame, w_in, w_out, joint):
    tokens = ROWS * COLS
    any_spec = pl.BlockSpec(memory_space=pltpu.HBM)
    out = jax.ShapeDtypeStruct((16, 16, D), BF16)
    return pl.pallas_call(
        encode_kernel,
        name="encode",
        in_specs=[pl.BlockSpec(memory_space=pltpu.SMEM)] + [any_spec] * 4,
        out_shape=(out, out),
        scratch_shapes=[
            pltpu.VMEM((tokens, D), BF16),
            pltpu.VMEM((D, D), BF16),
            pltpu.VMEM((D, D), BF16),
            pltpu.VMEM((D, D), BF16),
            pltpu.VMEM((tokens, D), F32),
            pltpu.SemaphoreType.DMA((4,)),
        ],
        compiler_params=pltpu.CompilerParams(vmem_limit_bytes=24 << 20),
        cost_estimate=pl.CostEstimate(flops=2 * tokens * D * (3 * D + tokens), bytes_accessed=6_000_000, transcendentals=tokens * D),
    )(chosen, *map(in_hbm, (frame, w_in, w_out, joint)))


def attend_kernel(shift_ref, up_ref, own_ref, down_ref, mine_ref, other_ref, strip_ref, w0_hbm, wq_hbm, wkv_hbm, wo_hbm, out_ref, bias_ref, stream_ref, normed_ref, qkv_ref, mixed_ref, w0, wqkv, wo, sems):
    copies = [
        pltpu.make_async_copy(w0_hbm.at[pl.ds(0, D), :], w0, sems.at[0]),
        pltpu.make_async_copy(wq_hbm, wqkv.at[:, :D], sems.at[1]),
        pltpu.make_async_copy(wkv_hbm, wqkv.at[:, D:], sems.at[2]),
        pltpu.make_async_copy(wo_hbm, wo, sems.at[3]),
    ]
    for c in copies:
        c.start()
    shift = shift_ref[0]
    core = axis_index("core")
    band = axis_index("lat")
    last = NLAT // ROWS - 1
    pairs = H // 2
    for h in range(H):
        for r in range(WIN):
            at = WIN * (WIN - 1 - r)
            bias_ref[h // 2, WIN * r : WIN * (r + 1), (h % 2) * HD : (h % 2 + 1) * HD] = strip_ref[h, :, at : at + HD]
    row, col = window_place(256, shift)
    order = one_hot(row * COLS + col, 256)
    tokens = jnp.concatenate([up_ref[...], own_ref[...], down_ref[...]], axis=0)
    copies[0].wait()
    noisy = dot(tokens, w0[...])

    def block(half, slot):
        mine, other = (ref[:, slot * 8 : slot * 8 + 8, :].astype(F32).reshape(128, D) for ref in (mine_ref, other_ref))
        return jnp.where(core == half, mine, other)

    for g, (low, high) in enumerate((((1, 2), (0, 0)), ((0, 1), (1, 1)), ((1, 0), (0, 2)))):
        rows = slice(g * 256, (g + 1) * 256)
        stream = (noisy[rows] + jnp.concatenate([block(*low), block(*high)], axis=0)).astype(BF16)
        stream_ref[rows, :] = stream
        normed_ref[rows, :] = dot(order, normalised(stream.astype(F32))).astype(BF16)
    copies[1].wait()
    copies[2].wait()
    for n in range(3):
        cols = slice(n * D, (n + 1) * D)
        made = dot(normed_ref[...], wqkv[:, cols])
        qkv_ref[:, cols] = (made * HD ** (-0.5) if n == 0 else made).astype(BF16)
    low = lax.broadcasted_iota(jnp.int32, (64, 128), 1) < HD
    key_row = lax.broadcasted_iota(jnp.int32, (64, 128), 0)

    def window(w, carry):
        rows = pl.ds(pl.multiple_of(w * 64, 64), 64)
        hide_top = jnp.logical_and(w < 4, band == 0)
        hide_end = jnp.logical_and(w >= 8, band == last)
        first = jnp.where(hide_top, 32, 0)
        end = jnp.where(hide_end, 32, 64)
        seen = jnp.logical_and(key_row >= first, key_row < end)
        scores = []
        for p in range(pairs):
            q = qkv_ref[rows, p * 128 : (p + 1) * 128]
            k = qkv_ref[rows, D + p * 128 : D + (p + 1) * 128]
            zero = jnp.zeros_like(q)
            both = jnp.concatenate([jnp.where(low, q, zero), jnp.where(low, zero, q)], axis=0)
            scores.append(dot_nt(k, both))
        scores = [jnp.where(seen, s + bias_ref[p], -1e30) for p, s in enumerate(scores)]
        tops = [jnp.max(s, axis=0, keepdims=True) for s in scores]
        weights = [jnp.exp(s - m) for s, m in zip(scores, tops)]
        sums = [1.0 / jnp.sum(e, axis=0, keepdims=True) for e in weights]
        probs = [(e * i).astype(BF16) for e, i in zip(weights, sums)]
        got = [dot_tn(probs[p], qkv_ref[rows, 2 * D + p * 128 : 2 * D + (p + 1) * 128]) for p in range(pairs)]
        for p in range(pairs):
            mixed_ref[rows, p * 128 : (p + 1) * 128] = jnp.where(low, got[p][:64], got[p][64:]).astype(BF16)
        return carry

    lax.fori_loop(0, 4 * GROUPS, window, 0, unroll=2)
    t = row_ids(128)
    moved = (t % COLS + shift) % COLS
    base = (moved // WIN) * 64 + (t // COLS) * WIN + moved % WIN
    for b in range(4):
        g, first = divmod(4 * b + 4, WIN)
        back = one_hot(base + first * WIN, 256)
        mixed = dot(back, mixed_ref[g * 256 : (g + 1) * 256, :]).astype(BF16)
        normed_ref[b * 128 : (b + 1) * 128, :] = mixed
    copies[3].wait()
    tokens = ROWS * COLS
    out_ref[...] = (stream_ref[EDGE : EDGE + tokens, :].astype(F32) + dot(normed_ref[:tokens, :], wo[...])).astype(BF16)


def attend(shift, up, own, down, mine, other, strip, joint, wq, wkv, wo):
    args = (up, own, down, mine, other, strip)
    return pl.pallas_call(
        attend_kernel,
        name="attend",
        in_specs=[
            pl.BlockSpec(memory_space=pltpu.SMEM),
            *(pl.BlockSpec(memory_space=pltpu.VMEM) for _ in args),
            *(pl.BlockSpec(memory_space=pltpu.HBM) for _ in range(4)),
        ],
        out_specs=pl.BlockSpec(memory_space=pltpu.VMEM),
        out_shape=jax.ShapeDtypeStruct((ROWS * COLS, D), BF16),
        scratch_shapes=[
            pltpu.VMEM((H // 2, 64, 128), F32),
            pltpu.VMEM((768, D), BF16),
            pltpu.VMEM((768, D), BF16),
            pltpu.VMEM((768, 3 * D), BF16),
            pltpu.VMEM((768, D), BF16),
            pltpu.VMEM((D, D), BF16),
            pltpu.VMEM((D, 3 * D), BF16),
            pltpu.VMEM((D, D), BF16),
            pltpu.SemaphoreType.DMA((4,)),
        ],
        compiler_params=pltpu.CompilerParams(vmem_limit_bytes=36 << 20),
        cost_estimate=pl.CostEstimate(flops=2 * 768 * D * 6 * D, bytes_accessed=10_000_000, transcendentals=768 * 64 * 12),
    )(shift, *args, *map(in_hbm, (joint, wq, wkv, wo)))


def forward_kernel(keep, att_ref, *refs):
    ups = refs[0:4]
    downs = refs[4:8]
    out_ref, total = refs[8:]
    unit = ups[0].shape[1]
    x = att_ref[...].astype(F32)
    second = normalised(x)
    for n in range(2):
        rings = (2 * n, 2 * n + 1)
        up = jnp.concatenate([ups[i][...].reshape(4 * unit, D) for i in rings], axis=0)
        hidden = jax.nn.gelu(dot_nt(second, up)).astype(BF16)
        down = jnp.concatenate([downs[j][i] for i in rings for j in range(4)], axis=0)
        part = dot(hidden, down)
        if n == 0:
            total[...] = x + part if keep else part
        else:
            out_ref[...] = (total[...] + part).astype(out_ref.dtype)


def feed_forward(keep, att, ups, downs):
    tokens = ROWS * COLS
    vmem = pl.BlockSpec(memory_space=pltpu.VMEM)
    return pl.pallas_call(
        lambda *refs: forward_kernel(keep, *refs),
        name="feed_forward_own" if keep else "feed_forward_partner",
        in_specs=[vmem] * 9,
        out_specs=vmem,
        out_shape=jax.ShapeDtypeStruct((tokens, D), F32 if keep else BF16),
        scratch_shapes=[pltpu.VMEM((tokens, D), F32)],
        compiler_params=pltpu.CompilerParams(vmem_limit_bytes=20 << 20),
        cost_estimate=pl.CostEstimate(flops=2 * tokens * D * FF, bytes_accessed=6_000_000, transcendentals=tokens * FF // 2),
    )(att, *ups, *downs)


def swap(x, axis):
    return lax.ppermute(x, axis, [(0, 1), (1, 0)])


def ring_from_all(mine, axis):
    on = [(i, (i + 1) % 4) for i in range(4)]
    back = [(i, (i - 1) % 4) for i in range(4)]
    behind = lax.ppermute(mine, axis, on)
    ahead = lax.ppermute(mine, axis, back)
    return [mine, behind, ahead, lax.ppermute(behind, axis, on)]


def row_from_all(mine, axis):
    moves = (1, -1, 2)
    got = [lax.ppermute(mine, axis, [(i, (i + by) % 4) for i in range(4)]) for by in moves]
    return jnp.stack([mine, *got], axis=0)


def gathered_weights(expand, reduce):
    n = expand.shape[0]
    across = swap(jnp.concatenate([expand, reduce], axis=0), "mz")
    ups = row_from_all(jnp.concatenate([expand, across[:n]], axis=0), "mx")
    downs = row_from_all(jnp.concatenate([reduce, across[n:]], axis=0), "my")
    return ring_from_all(ups, "my"), ring_from_all(downs, "mx")


def strip_choice():
    lane = lax.optimization_barrier(jnp.arange(WIN * 15 * WIN))
    key_col = lane // (15 * WIN)
    block = lane // WIN % 15
    wanted = (14 - block) * 15 + key_col - lane % WIN + 7
    return jnp.where(jnp.arange(225)[:, None] == wanted[None, :], 1.0, 0.0).astype(F32)


def body(
    noisy_latents,
    frames,
    encoder_members,
    window_shift,
    encoder_in,
    encoder_out,
    joint_weight,
    query_weight,
    keyvalue_weight,
    output_weight,
    position_bias,
    expand_weight,
    reduce_weight,
):
    tokens = ROWS * COLS
    bands = lax.axis_size("lat")
    noisy = noisy_latents.reshape(tokens, D)
    to_next = [(i, (i + 1) % bands) for i in range(bands)]
    to_last = [(i, (i - 1) % bands) for i in range(bands)]

    keep, send = encode(encoder_members, frames.reshape(tokens, D), encoder_in, encoder_out, joint_weight)
    ups, downs = gathered_weights(expand_weight, reduce_weight)
    noisy_up = lax.ppermute(noisy[tokens - EDGE :], "lat", to_next)
    noisy_down = lax.ppermute(noisy[:EDGE], "lat", to_last)

    mine = keep + swap(send, "core")
    spread = lax.all_to_all(mine, PLANE, 0, 0, tiled=True)
    part = jnp.sum(spread.astype(F32), axis=0).astype(BF16)
    pairs = [(l, (l - 1) % bands) for l in range(bands)] + [(bands + l, bands + (l + 1) % bands) for l in range(bands)]
    part = jnp.concatenate([part, lax.ppermute(part[:8], ("core", "lat"), pairs)], axis=0)
    part = part + swap(part, "mz")
    wide = jnp.broadcast_to(part[None], (16, *part.shape))
    mine = lax.all_to_all(wide, PLANE, 0, 0, tiled=True)
    other = swap(mine, "core")

    strip = jnp.dot(position_bias, strip_choice(), precision=lax.Precision.HIGHEST, preferred_element_type=F32)
    strip = strip.reshape(H, WIN, 15 * WIN)
    attended = attend(
        window_shift, noisy_up, noisy, noisy_down, mine, other, strip, joint_weight, query_weight, keyvalue_weight, output_weight
    )
    partner = swap(attended, "core")
    own = feed_forward(True, attended, ups, downs)
    theirs = feed_forward(False, partner, ups, downs)
    back = swap(theirs, "core")
    return (own + back.astype(F32)).astype(BF16).reshape(noisy_latents.shape)


def solution(mesh):
    finer = Mesh(mesh.devices.reshape(4, 4, 2, 2, mesh.shape["lat"]), (*MEMBER, "lat"))
    placed = (
        P(MEMBER, "lat", None, None),
        P(MEMBER, "lat", None, None),
        *([P()] * 9),
        P(MEMBER, None),
        P(MEMBER, None),
    )
    return jax.shard_map(
        body,
        mesh=finer,
        in_specs=placed,
        out_specs=P(MEMBER, "lat", None, None),
        check_vma=False,
    )
```

```python
import jax
import jax.numpy as jnp
from jax import lax
from jax.experimental import pallas as pl
from jax.experimental.pallas import tpu as pltpu
from jax.sharding import Mesh
from jax.sharding import PartitionSpec as P

HD = 64
WIN = 8
D = 768
H = 12
FF = 3072
ROWS = 16
COLS = 32
NLAT = 64
EDGE = WIN // 2 * COLS
MEMBER = ("mx", "my", "mz", "core")
PLANE = ("mx", "my")
EPS = 1e-06
F32 = jnp.float32
BF16 = jnp.bfloat16
axis_index = lax.axis_index


def in_hbm(x):
    return pltpu.with_memory_space_constraint(x, pltpu.HBM)


def dot(a, b):
    return jnp.dot(a, b, preferred_element_type=F32)


def dot_nt(a, b):
    return lax.dot_general(a, b, (((1,), (1,)), ((), ())), preferred_element_type=F32)


def dot_tn(a, b):
    return lax.dot_general(a, b, (((0,), (0,)), ((), ())), preferred_element_type=F32)


def normalised(x):
    scale = lax.rsqrt(jnp.mean(x * x, axis=-1, keepdims=True) + EPS)
    return (x * scale).astype(BF16)


def one_hot(wanted, width):
    lanes = lax.broadcasted_iota(jnp.int32, (wanted.shape[0], width), 1)
    return jnp.where(lanes == wanted, 1.0, 0.0).astype(BF16)


def row_ids(count):
    return lax.broadcasted_iota(jnp.int32, (count, 1), 0)


def window_place(count, shift):
    t = row_ids(count)
    row = (t // WIN) % WIN
    col = ((t // (WIN * WIN)) * WIN + t % WIN - shift + COLS) % COLS
    return row, col


def encode_kernel(chosen, frame_hbm, in_hbm, out_hbm, joint_hbm, keep_ref, send_ref, frame, w_in, w_out, w_slot, term_ref, sems):
    own_core = axis_index("core")
    member = axis_index(MEMBER)
    is_second = member == chosen[1]
    is_source = jnp.logical_or(member == chosen[0], is_second)
    slot = jnp.where(is_second, 2, 1)
    copies = [
        pltpu.make_async_copy(frame_hbm, frame, sems.at[0]),
        pltpu.make_async_copy(in_hbm, w_in, sems.at[1]),
        pltpu.make_async_copy(out_hbm, w_out, sems.at[2]),
        pltpu.make_async_copy(joint_hbm.at[pl.ds(pl.multiple_of(slot * D, D), D), :], w_slot, sems.at[3]),
    ]
    for c in copies:
        c.start()
    copies[0].wait()
    copies[1].wait()
    hidden = jax.nn.gelu(dot(frame[...], w_in[...])).astype(BF16)
    copies[2].wait()
    condition = dot(hidden, w_out[...]).astype(BF16)
    copies[3].wait()
    term = dot(condition, w_slot[...])
    term_ref[...] = jnp.where(is_source, term, 0.0)
    for half, out_ref in ((own_core, keep_ref), (1 - own_core, send_ref)):
        for slot, start in enumerate((jnp.where(half == 0, 0, 384), jnp.where(half == 0, 128, 256))):
            block = term_ref[pl.ds(pl.multiple_of(start, 128), 128), :]
            out_ref[:, slot * 8 : slot * 8 + 8, :] = block.reshape(16, 8, D).astype(BF16)


def encode(chosen, frame, w_in, w_out, joint):
    tokens = ROWS * COLS
    any_spec = pl.BlockSpec(memory_space=pltpu.HBM)
    out = jax.ShapeDtypeStruct((16, 16, D), BF16)
    return pl.pallas_call(
        encode_kernel,
        name="encode",
        in_specs=[pl.BlockSpec(memory_space=pltpu.SMEM)] + [any_spec] * 4,
        out_shape=(out, out),
        scratch_shapes=[
            pltpu.VMEM((tokens, D), BF16),
            pltpu.VMEM((D, D), BF16),
            pltpu.VMEM((D, D), BF16),
            pltpu.VMEM((D, D), BF16),
            pltpu.VMEM((tokens, D), F32),
            pltpu.SemaphoreType.DMA((4,)),
        ],
        compiler_params=pltpu.CompilerParams(vmem_limit_bytes=24 << 20),
        cost_estimate=pl.CostEstimate(flops=2 * tokens * D * (3 * D + tokens), bytes_accessed=6_000_000, transcendentals=tokens * D),
    )(chosen, *map(in_hbm, (frame, w_in, w_out, joint)))


def attend_kernel(shift_ref, up_ref, own_ref, down_ref, mine_ref, other_ref, strip_ref, w0_hbm, wq_hbm, wkv_hbm, wo_hbm, out_ref, bias_ref, rim_bias_ref, stream_ref, normed_ref, query_ref, kv_ref, mixed_ref, w0, wq, wkv, wo, sems):
    copies = [
        pltpu.make_async_copy(w0_hbm.at[pl.ds(0, D), :], w0, sems.at[0]),
        pltpu.make_async_copy(wkv_hbm, wkv, sems.at[1]),
        pltpu.make_async_copy(wq_hbm, wq, sems.at[2]),
        pltpu.make_async_copy(wo_hbm, wo, sems.at[3]),
    ]
    for c in copies:
        c.start()
    shift = shift_ref[0]
    core = axis_index("core")
    band = axis_index("lat")
    last = NLAT // ROWS - 1
    for h in range(H):
        for r in range(WIN):
            at = WIN * (WIN - 1 - r)
            rows = slice(WIN * r, WIN * (r + 1))
            taken = strip_ref[h, :, at : at + HD]
            bias_ref[h // 2, rows, (h % 2) * HD : (h % 2 + 1) * HD] = taken
            lanes = slice((h % 4) * 32, (h % 4) * 32 + 32)
            upper, lower = taken[:, 32:], taken[:, :32]
            rim_bias_ref[0, h // 4, rows, lanes] = jnp.where(band == 0, -1e30, upper) if r < 4 else upper
            rim_bias_ref[1, h // 4, rows, lanes] = jnp.where(band == last, -1e30, lower) if r >= 4 else lower
    row, col = window_place(256, shift)
    order = one_hot(row * COLS + col, 256)
    tokens = jnp.concatenate([up_ref[...], own_ref[...], down_ref[...]], axis=0)
    copies[0].wait()
    noisy = dot(tokens, w0[...])

    def block(half, slot):
        mine, other = (ref[:, slot * 8 : slot * 8 + 8, :].astype(F32).reshape(128, D) for ref in (mine_ref, other_ref))
        return jnp.where(core == half, mine, other)

    for g, (low, high) in enumerate((((1, 2), (0, 0)), ((0, 1), (1, 1)), ((1, 0), (0, 2)))):
        rows = slice(g * 256, (g + 1) * 256)
        stream = (noisy[rows] + jnp.concatenate([block(*low), block(*high)], axis=0)).astype(BF16)
        stream_ref[rows, :] = stream
        normed_ref[rows, :] = dot(order, normalised(stream.astype(F32))).astype(BF16)
    copies[1].wait()
    for n in range(2):
        cols = slice(n * D, (n + 1) * D)
        kv_ref[:, cols] = dot(normed_ref[...], wkv[:, cols]).astype(BF16)
    own = [normed_ref[w * 64 + 32 : w * 64 + 64, :] for w in range(4)]
    own += [normed_ref[256:512, :]]
    own += [normed_ref[512 + w * 64 : 512 + w * 64 + 32, :] for w in range(4)]
    copies[2].wait()
    query_ref[...] = (dot(jnp.concatenate(own, axis=0), wq[...]) * HD ** (-0.5)).astype(BF16)

    def spread(q, heads):
        of_lane = lax.broadcasted_iota(jnp.int32, q.shape, 1) // HD
        return jnp.concatenate([jnp.where(of_lane == a, q, jnp.zeros_like(q)) for a in range(heads)], axis=0)

    def gathered(got, heads):
        count = got.shape[0] // heads
        of_lane = lax.broadcasted_iota(jnp.int32, (count, got.shape[1]), 1) // HD
        out = got[:count]
        for a in range(1, heads):
            out = jnp.where(of_lane == a, got[a * count : (a + 1) * count], out)
        return out.astype(BF16)

    def windows(w, carry):
        jobs = []
        mid = pl.ds(pl.multiple_of(128 + w * 64, 64), 64)
        keys = pl.ds(pl.multiple_of(256 + w * 64, 64), 64)
        for p in range(H // 2):
            jobs.append((mid, keys, p * 128, 2, bias_ref[p]))
        for side in range(2):
            few = pl.ds(pl.multiple_of(384 * side + w * 32, 32), 32)
            keys = pl.ds(pl.multiple_of(512 * side + w * 64, 64), 64)
            for n in range(H // 4):
                jobs.append((few, keys, n * 256, 4, rim_bias_ref[side, n]))
        scores = []
        for queries, keys, at, heads, bias in jobs:
            cols = slice(at, at + heads * HD)
            scores.append(dot_nt(kv_ref[keys, cols], spread(query_ref[queries, cols], heads)) + bias)
        tops = [jnp.max(s, axis=0, keepdims=True) for s in scores]
        weights = [jnp.exp(s - m) for s, m in zip(scores, tops)]
        sums = [1.0 / jnp.sum(e, axis=0, keepdims=True) for e in weights]
        probs = [(e * i).astype(BF16) for e, i in zip(weights, sums)]
        got = [dot_tn(p, kv_ref[keys, D + at : D + at + heads * HD]) for p, (_, keys, at, heads, _) in zip(probs, jobs)]
        for g, (queries, _, at, heads, _) in zip(got, jobs):
            mixed_ref[queries, at : at + heads * HD] = gathered(g, heads)
        return carry

    lax.fori_loop(0, 4, windows, 0)
    t = row_ids(128)
    moved = (t % COLS + shift) % COLS
    window, place = moved // WIN, t // COLS * WIN + moved % WIN
    few = one_hot(window * 32 + place, 128)
    parts = [dot(few, mixed_ref[:128, :])]
    parts += [dot(one_hot(window * 64 + place + 32 * n, 256), mixed_ref[128:384, :]) for n in range(2)]
    parts += [dot(few, mixed_ref[384:, :])]
    mixed = jnp.concatenate(parts, axis=0).astype(BF16)
    copies[3].wait()
    tokens = ROWS * COLS
    out_ref[...] = (stream_ref[EDGE : EDGE + tokens, :].astype(F32) + dot(mixed, wo[...])).astype(BF16)


def attend(shift, up, own, down, mine, other, strip, joint, wq, wkv, wo):
    args = (up, own, down, mine, other, strip)
    return pl.pallas_call(
        attend_kernel,
        name="attend",
        in_specs=[
            pl.BlockSpec(memory_space=pltpu.SMEM),
            *(pl.BlockSpec(memory_space=pltpu.VMEM) for _ in args),
            *(pl.BlockSpec(memory_space=pltpu.HBM) for _ in range(4)),
        ],
        out_specs=pl.BlockSpec(memory_space=pltpu.VMEM),
        out_shape=jax.ShapeDtypeStruct((ROWS * COLS, D), BF16),
        scratch_shapes=[
            pltpu.VMEM((H // 2, 64, 128), F32),
            pltpu.VMEM((2, H // 4, 64, 128), F32),
            pltpu.VMEM((768, D), BF16),
            pltpu.VMEM((768, D), BF16),
            pltpu.VMEM((ROWS * COLS, D), BF16),
            pltpu.VMEM((768, 2 * D), BF16),
            pltpu.VMEM((ROWS * COLS, D), BF16),
            pltpu.VMEM((D, D), BF16),
            pltpu.VMEM((D, D), BF16),
            pltpu.VMEM((D, 2 * D), BF16),
            pltpu.VMEM((D, D), BF16),
            pltpu.SemaphoreType.DMA((4,)),
        ],
        compiler_params=pltpu.CompilerParams(vmem_limit_bytes=36 << 20),
        cost_estimate=pl.CostEstimate(flops=2 * 768 * D * 6 * D, bytes_accessed=10_000_000, transcendentals=768 * 64 * 12),
    )(shift, *args, *map(in_hbm, (joint, wq, wkv, wo)))


def forward_kernel(keep, att_ref, *refs):
    ups = refs[0:4]
    downs = refs[4:8]
    out_ref, total = refs[8:]
    unit = ups[0].shape[1]
    x = att_ref[...].astype(F32)
    second = normalised(x)
    for n in range(2):
        rings = (2 * n, 2 * n + 1)
        up = jnp.concatenate([ups[i][...].reshape(4 * unit, D) for i in rings], axis=0)
        hidden = jax.nn.gelu(dot_nt(second, up)).astype(BF16)
        down = jnp.concatenate([downs[j][i] for i in rings for j in range(4)], axis=0)
        part = dot(hidden, down)
        if n == 0:
            total[...] = x + part if keep else part
        else:
            out_ref[...] = (total[...] + part).astype(out_ref.dtype)


def feed_forward(keep, att, ups, downs):
    tokens = ROWS * COLS
    vmem = pl.BlockSpec(memory_space=pltpu.VMEM)
    return pl.pallas_call(
        lambda *refs: forward_kernel(keep, *refs),
        name="feed_forward_own" if keep else "feed_forward_partner",
        in_specs=[vmem] * 9,
        out_specs=vmem,
        out_shape=jax.ShapeDtypeStruct((tokens, D), F32 if keep else BF16),
        scratch_shapes=[pltpu.VMEM((tokens, D), F32)],
        compiler_params=pltpu.CompilerParams(vmem_limit_bytes=20 << 20),
        cost_estimate=pl.CostEstimate(flops=2 * tokens * D * FF, bytes_accessed=6_000_000, transcendentals=tokens * FF // 2),
    )(att, *ups, *downs)


def swap(x, axis):
    return lax.ppermute(x, axis, [(0, 1), (1, 0)])


def ring_from_all(mine, axis):
    on = [(i, (i + 1) % 4) for i in range(4)]
    back = [(i, (i - 1) % 4) for i in range(4)]
    behind = lax.ppermute(mine, axis, on)
    ahead = lax.ppermute(mine, axis, back)
    return [mine, behind, ahead, lax.ppermute(behind, axis, on)]


def row_from_all(mine, axis):
    moves = (1, -1, 2)
    got = [lax.ppermute(mine, axis, [(i, (i + by) % 4) for i in range(4)]) for by in moves]
    return jnp.stack([mine, *got], axis=0)


def gathered_weights(expand, reduce):
    n = expand.shape[0]
    across = swap(jnp.concatenate([expand, reduce], axis=0), "mz")
    ups = row_from_all(jnp.concatenate([expand, across[:n]], axis=0), "mx")
    downs = row_from_all(jnp.concatenate([reduce, across[n:]], axis=0), "my")
    return ring_from_all(ups, "my"), ring_from_all(downs, "mx")


def strip_choice():
    lane = lax.optimization_barrier(jnp.arange(WIN * 15 * WIN))
    key_col = lane // (15 * WIN)
    block = lane // WIN % 15
    wanted = (14 - block) * 15 + key_col - lane % WIN + 7
    return jnp.where(jnp.arange(225)[:, None] == wanted[None, :], 1.0, 0.0).astype(F32)


def body(
    noisy_latents,
    frames,
    encoder_members,
    window_shift,
    encoder_in,
    encoder_out,
    joint_weight,
    query_weight,
    keyvalue_weight,
    output_weight,
    position_bias,
    expand_weight,
    reduce_weight,
):
    tokens = ROWS * COLS
    bands = lax.axis_size("lat")
    noisy = noisy_latents.reshape(tokens, D)
    to_next = [(i, (i + 1) % bands) for i in range(bands)]
    to_last = [(i, (i - 1) % bands) for i in range(bands)]

    keep, send = encode(encoder_members, frames.reshape(tokens, D), encoder_in, encoder_out, joint_weight)
    ups, downs = gathered_weights(expand_weight, reduce_weight)
    noisy_up = lax.ppermute(noisy[tokens - EDGE :], "lat", to_next)
    noisy_down = lax.ppermute(noisy[:EDGE], "lat", to_last)

    handed = swap(send, "core")
    mine = keep + handed
    spread = lax.all_to_all(mine, PLANE, 0, 0, tiled=True)
    part = jnp.sum(spread.astype(F32), axis=0).astype(BF16)
    pairs = [(l, (l - 1) % bands) for l in range(bands)] + [(bands + l, bands + (l + 1) % bands) for l in range(bands)]
    part = jnp.concatenate([part, lax.ppermute(part[:8], ("core", "lat"), pairs)], axis=0)
    part = part + swap(part, "mz")
    wide = jnp.broadcast_to(part[None], (16, *part.shape))
    mine = lax.all_to_all(wide, PLANE, 0, 0, tiled=True)
    other = swap(mine, "core")

    strip = jnp.dot(position_bias, strip_choice(), precision=lax.Precision.HIGHEST, preferred_element_type=F32)
    strip = strip.reshape(H, WIN, 15 * WIN)
    attended = attend(
        window_shift, noisy_up, noisy, noisy_down, mine, other, strip, joint_weight, query_weight, keyvalue_weight, output_weight
    )
    partner = swap(attended, "core")
    own = feed_forward(True, attended, ups, downs)
    theirs = feed_forward(False, partner, ups, downs)
    back = swap(theirs, "core")
    return (own + back.astype(F32)).astype(BF16).reshape(noisy_latents.shape)


def solution(mesh):
    finer = Mesh(mesh.devices.reshape(4, 4, 2, 2, mesh.shape["lat"]), (*MEMBER, "lat"))
    placed = (
        P(MEMBER, "lat", None, None),
        P(MEMBER, "lat", None, None),
        *([P()] * 9),
        P(MEMBER, None),
        P(MEMBER, None),
    )
    return jax.shard_map(
        body,
        mesh=finer,
        in_specs=placed,
        out_specs=P(MEMBER, "lat", None, None),
        check_vma=False,
    )
```
